32 devices in a mesh: grp: 4 (over z), row: 8 (over y, x, core).
Axes of the slice: x: 2, y: 2, z: 4, core: 2. Of those that a mesh axis runs over, the one named last changes fastest.
Arguments:
- basis: float32 [8192, 1024], P(('grp', 'row')), may hold values from -40 to 40
- block: float32 [8192, 512], P(('grp', 'row')), may hold values from -600 to 600
- counts: int32 [4, 8], P('grp', 'row'), may hold values from 128 to 256, as said below
Outputs:
- new_block: float32 [8192, 512], P(('grp', 'row'))
- factor: float32 [512, 512], replicated
The draws below stay inside these ranges and needn't reach their ends.
Inputs may be any that keep to these rules, and one draw needn't show every extreme that they name: `counts`: each device's live rows are a multiple of 128, at most 256; one device holds exactly 256.
All inputs are finite; a program needn't handle non-finite values.
Results may differ from the reference program's by a relative error of at most 0.0003.
Values sent between devices are 32-bit elements; how exact they have to be, the bound alone decides.
A program may use at most 64 MiB of HBM per device.

```python
import math
import jax
import jax.numpy as jnp
from jax import lax

M = 1024
K = 512
CAP = 256
ROWS_ALL = 8192
N_GRP = 4
N_ROW = 8


def draw_counts(key, part):
    tiles = CAP // 128
    upper = max(2, 2 * tiles // 3)
    base = jax.random.randint(key, (N_GRP * N_ROW,), 1, upper)
    heavy = jax.random.randint(jax.random.fold_in(key, 7), (), 0, N_GRP * N_ROW)
    places = jnp.arange(N_GRP * N_ROW, dtype=jnp.int32)
    filled = jnp.where(places == heavy, tiles, base)
    return (filled * 128).reshape(N_GRP, N_ROW).astype(jnp.int32)


def live_rows(key, part):
    filled = draw_counts(key, part).reshape(-1)
    positions = jnp.arange(ROWS_ALL, dtype=jnp.int32)
    limit = filled[positions // CAP]
    return (positions % CAP < limit).astype(jnp.float32)[:, None]


def basis_span(key, part):
    live = live_rows(key, part)
    raw = jax.random.normal(jax.random.fold_in(key, 101), (ROWS_ALL, M), jnp.float32) * live
    orthonormal, upper_part = jnp.linalg.qr(raw)
    orthonormal = orthonormal * live * math.sqrt(ROWS_ALL)
    tilt = jnp.eye(M, dtype=jnp.float32) + 0.032 * jax.random.normal(jax.random.fold_in(key, 102), (M, M), jnp.float32) / math.sqrt(M)
    spanned = jnp.dot(orthonormal, tilt, precision=lax.Precision.HIGHEST) * live
    return (spanned, live)


def draw_basis(key, part):
    spanned, live = basis_span(key, part)
    filler = 1.7 * jax.random.normal(jax.random.fold_in(key, 103), (ROWS_ALL, M), jnp.float32)
    return jnp.clip(spanned + (1.0 - live) * filler, -40.0, 40.0)


def draw_block(key, part):
    spanned, live = basis_span(key, part)
    amounts = 30.0 * jax.random.normal(jax.random.fold_in(key, 201), (M, K), jnp.float32) / math.sqrt(M)
    along = jnp.dot(spanned, amounts, precision=lax.Precision.HIGHEST)
    rough = jax.random.normal(jax.random.fold_in(key, 202), (ROWS_ALL, K), jnp.float32)
    column_scale = jnp.exp(jax.random.uniform(jax.random.fold_in(key, 203), (K,), jnp.float32, math.log(0.5), math.log(5.0)))
    mixing = jnp.eye(K, dtype=jnp.float32) + 0.3 * jax.random.normal(jax.random.fold_in(key, 204), (K, K), jnp.float32) / math.sqrt(K)
    off_span = jnp.dot(rough * column_scale[None, :], mixing, precision=lax.Precision.HIGHEST)
    filler = jax.random.normal(jax.random.fold_in(key, 205), (ROWS_ALL, K), jnp.float32)
    return jnp.clip(live * (along + off_span) + (1.0 - live) * filler, -600.0, 600.0)


def setup_inputs(seed: int = 0) -> dict:
    seeds = jax.random.split(jax.random.key(seed), 4)
    return {
        "basis": draw_basis(jax.random.fold_in(seeds[3], 71), 0),
        "block": draw_block(jax.random.fold_in(seeds[3], 71), 0),
        "counts": draw_counts(jax.random.fold_in(seeds[3], 71), 0),
    }


def reference(basis, block, counts):
    total = basis.shape[0]
    positions = jnp.arange(total, dtype=jnp.int32)
    owner = positions // CAP
    limit = counts.reshape(-1).astype(jnp.int32)[owner]
    live = (positions % CAP < limit).astype(basis.dtype)[:, None]
    basis_live = basis * live
    block_live = block * live
    coeffs = jnp.dot(basis_live.T, block_live, precision=lax.Precision.HIGHEST) / ROWS_ALL
    first_pass = block_live - jnp.dot(basis_live, coeffs, precision=lax.Precision.HIGHEST)
    correction = jnp.dot(basis_live.T, first_pass, precision=lax.Precision.HIGHEST) / ROWS_ALL
    residual = first_pass - jnp.dot(basis_live, correction, precision=lax.Precision.HIGHEST)
    gram = jnp.dot(residual.T, residual, precision=lax.Precision.HIGHEST) / ROWS_ALL
    lower_factor = jnp.linalg.cholesky(gram)
    new_block = lax.linalg.triangular_solve(lower_factor, residual, left_side=False, lower=True, transpose_a=True)
    return (new_block, lower_factor.T)
```

```python
import functools
import math

import jax
import jax.numpy as jnp
from jax import lax
from jax.experimental import pallas as pl
from jax.experimental.pallas import tpu as pltpu
from jax.sharding import PartitionSpec as P

HIGHEST = lax.Precision.HIGHEST
MESH = pl.DeviceIdType.MESH
TILE = 128


def transposed_product(left, right):
    return lax.dot_general(
        left,
        right,
        (((0,), (0,)), ((), ())),
        precision=HIGHEST,
        preferred_element_type=jnp.float32,
    )


def matrix_product(left, right):
    return jnp.dot(left, right, precision=HIGHEST, preferred_element_type=jnp.float32)


def plane_sides(chips):
    side = math.isqrt(chips)
    while chips % side:
        side -= 1
    return chips // side, side


class Piece:
    def __init__(self, tiles, order, chips):
        self.used = tiles
        self.tiles = -(-tiles // chips) * chips
        self.order = order


def make_plan(basis_columns, block_columns, sizes):
    chips = sizes["x"] * sizes["y"] * sizes["z"]
    block = basis_columns // 4
    half = block_columns // 2
    square = block * block // 1024
    corner = half * half // 1024
    forward, backward = ("x", "y", "z"), ("y", "x", "z")
    basis_gram = [
        Piece(2 * (square - square // 4), forward, chips),
        Piece(square, backward, chips),
        Piece(square, backward, chips),
        Piece(square, forward, chips),
    ]
    coeffs = [Piece(block * half // 1024, (forward, backward)[i % 2], chips) for i in range(4)]
    gram = [Piece(corner - corner // 4, forward, chips), Piece(corner // 2, backward, chips)]
    place = dict(copy=0, source=0, held=0, partial=0)
    for group in (basis_gram, coeffs, gram):
        offset = 0
        for piece in group:
            piece.offset = offset
            offset += piece.tiles
            piece.source = place["source"]
            place["source"] += piece.tiles
            piece.stages = []
            size = piece.tiles
            for axis in piece.order:
                count = sizes[axis]
                size //= count
                stage = dict(axis=axis, size=size, held=place["held"], partial=place["partial"])
                stage["scatter"] = place["copy"]
                stage["gather"] = place["copy"] + count - 1
                place["copy"] += 2 * (count - 1)
                place["held"] += (count - 1) * size
                place["partial"] += size
                piece.stages.append(stage)
            piece.partner = place["copy"]
            place["copy"] += 1
    return basis_gram, coeffs, gram, place


def pieces_to_tiles(value):
    rows, cols = value.shape
    return [value[:, i : i + TILE].reshape(rows // 8, 8, TILE) for i in range(0, cols, TILE)]


def orthogonalize_kernel(
    plan,
    sizes,
    weight,
    counts_ref,
    basis_ref,
    block_ref,
    residual_ref,
    gram_ref,
    basis_all,
    block_half,
    block_send,
    source,
    held,
    partial,
    basis_gram_tiles,
    coeffs_tiles,
    gram_tiles,
    operator,
    correction,
    residual,
    send_sem,
    recv_sem,
    extra_send,
    extra_recv,
):
    basis_gram, coeffs, gram, _ = plan
    slots = basis_ref.shape[0]
    columns = basis_ref.shape[1]
    half = block_ref.shape[1] // 2
    block = columns // 4

    row = lax.axis_index("row")
    core = lax.rem(row, 2)
    chip = lax.div(row, 2)
    me = {"x": lax.rem(chip, sizes["x"]), "y": lax.div(chip, sizes["x"]), "z": lax.axis_index("grp")}
    partner = {"row": row + 1 - 2 * core}

    def peer(axis, k):
        other = lax.rem(me[axis] + k, sizes[axis])
        if axis == "z":
            return {"grp": other}
        x, y = (other, me["y"]) if axis == "x" else (me["x"], other)
        return {"row": (y * sizes["x"] + x) * 2 + core}

    barrier = pltpu.get_barrier_semaphore()
    pl.semaphore_signal(barrier, inc=1, device_id=partner, device_id_type=MESH)
    for axis in sizes:
        for k in range(1, sizes[axis]):
            pl.semaphore_signal(barrier, inc=1, device_id=peer(axis, k), device_id_type=MESH)
    sent = []

    def start(source_ref, target_ref, sends, recvs, device):
        copy = pltpu.make_async_remote_copy(
            src_ref=source_ref,
            dst_ref=target_ref,
            send_sem=sends,
            recv_sem=recvs,
            device_id=device,
            device_id_type=MESH,
        )
        copy.start()
        sent.append(copy)
        return copy

    live = lax.broadcasted_iota(jnp.int32, (slots, 1), 0) < counts_ref[0, 0]
    mine = pl.ds(pl.multiple_of(core * slots, 8), slots)
    near = pl.ds(pl.multiple_of(core * half, TILE), half)
    far = pl.ds(pl.multiple_of((1 - core) * half, TILE), half)
    basis_all[mine, :] = jnp.where(live, basis_ref[...], 0.0)
    block_send[...] = jnp.where(live, block_ref[:, far], 0.0)
    block_half[mine, :] = jnp.where(live, block_ref[:, near], 0.0)
    pl.semaphore_wait(barrier, 1 + sum(size - 1 for size in sizes.values()))
    shared = [
        start(basis_all.at[mine], basis_all.at[mine], extra_send.at[0], extra_recv.at[0], partner),
        start(block_send, block_half.at[mine], extra_send.at[1], extra_recv.at[1], partner),
    ]

    def position(piece, depth):
        offset = 0
        for stage in piece.stages[:depth]:
            offset = offset + me[stage["axis"]] * stage["size"]
        return offset

    def scatter(piece, depth):
        stage = piece.stages[depth]
        axis, size = stage["axis"], stage["size"]
        if depth == 0:
            base, ref = piece.source, source
        else:
            base, ref = piece.stages[depth - 1]["partial"], partial
        piece.waiting = []
        for k in range(1, sizes[axis]):
            chunk = lax.rem(me[axis] + k, sizes[axis]) * size
            index = stage["scatter"] + k - 1
            piece.waiting.append(
                start(
                    ref.at[pl.ds(base + chunk, size)],
                    held.at[pl.ds(stage["held"] + (k - 1) * size, size)],
                    send_sem.at[index],
                    recv_sem.at[index],
                    peer(axis, k),
                )
            )

    def reduced(piece, depth):
        stage = piece.stages[depth]
        axis, size = stage["axis"], stage["size"]
        if depth == 0:
            base, ref = piece.source, source
        else:
            base, ref = piece.stages[depth - 1]["partial"], partial
        for copy in piece.waiting:
            copy.wait_recv()
        total = ref[pl.ds(base + me[axis] * size, size)]
        for k in range(sizes[axis] - 1):
            total = total + held[pl.ds(stage["held"] + k * size, size)]
        return total

    def gather(piece, depth):
        stage = piece.stages[depth]
        axis = stage["axis"]
        place = piece.out.at[pl.ds(piece.offset + position(piece, depth + 1), stage["size"])]
        piece.waiting = []
        for k in range(1, sizes[axis]):
            index = stage["gather"] + k - 1
            piece.waiting.append(start(place, place, send_sem.at[index], recv_sem.at[index], peer(axis, k)))

    def advance(piece, step):
        if step == 0:
            blocks = piece.produce()
            offset = piece.source
            for value in blocks:
                source[pl.ds(offset, value.shape[0])] = value
                offset += value.shape[0]
            if piece.used < piece.tiles:
                source[pl.ds(offset, piece.tiles - piece.used)] = jnp.zeros(
                    (piece.tiles - piece.used, 8, TILE), jnp.float32
                )
            scatter(piece, 0)
        elif step < 3:
            stage = piece.stages[step - 1]
            partial[pl.ds(stage["partial"], stage["size"])] = reduced(piece, step - 1)
            scatter(piece, step)
        elif step == 3:
            size = piece.stages[2]["size"]
            piece.out[pl.ds(piece.offset + position(piece, 3), size)] = reduced(piece, 2)
            gather(piece, 2)
        elif step < 6:
            for copy in piece.waiting:
                copy.wait_recv()
            gather(piece, 5 - step)
        elif step == 6:
            for copy in piece.waiting:
                copy.wait_recv()
            if piece.shared:
                place = piece.out.at[pl.ds(piece.offset, piece.tiles)]
                index = piece.partner
                piece.waiting = [start(place, place, send_sem.at[index], recv_sem.at[index], partner)]
            else:
                piece.consume()
        elif step == 7 and piece.shared:
            for copy in piece.waiting:
                copy.wait_recv()
            piece.consume()

    def run(pairs):
        for tick in range(len(pairs) + 7):
            for index, pair in enumerate(pairs):
                if 0 <= tick - index <= 7:
                    for piece in pair:
                        advance(piece, tick - index)

    def lanes(index, width):
        return pl.ds(pl.multiple_of(index * width, TILE), width)

    first, second = 2 * core, 2 * core + 1

    def basis_product(left, right):
        return transposed_product(basis_all[:, lanes(left, block)], basis_all[:, lanes(right, block)]) * weight

    def upper_tiles(value):
        middle = value.shape[0] // 2
        return pieces_to_tiles(value[:middle]) + pieces_to_tiles(value[middle:, middle:])

    def square_at(ref, offset, rows, cols):
        parts = [
            ref[pl.ds(offset + i * (rows // 8), rows // 8)].reshape(rows, TILE) for i in range(cols // TILE)
        ]
        return jnp.concatenate(parts, axis=1)

    def upper_at(ref, offset, size):
        middle = size // 2
        top = square_at(ref, offset, middle, size)
        corner = square_at(ref, offset + middle * size // 1024, middle, middle)
        return top, corner

    square = block * block // 1024

    def put_diagonal(owner, offset, index):
        top, corner = upper_at(basis_gram_tiles.at[owner], offset, block)
        middle = block // 2
        whole = jnp.concatenate([top, jnp.concatenate([top[:, middle:].T, corner], axis=1)], axis=0)
        unit = lax.broadcasted_iota(jnp.int32, whole.shape, 0) == lax.broadcasted_iota(jnp.int32, whole.shape, 1)
        window = slice(index * block, (index + 1) * block)
        operator[window, window] = jnp.where(unit, 1.0, 0.0) - whole

    def put_square(owner, offset, left, right):
        whole = -square_at(basis_gram_tiles.at[owner], offset, block, block)
        rows, cols = slice(left * block, (left + 1) * block), slice(right * block, (right + 1) * block)
        operator[rows, cols] = whole
        operator[cols, rows] = whole.T

    def consume_diagonals():
        offset = basis_gram[0].offset
        for owner in range(2):
            put_diagonal(owner, offset, 2 * owner)
            put_diagonal(owner, offset + square - square // 4, 2 * owner + 1)

    def consume_square(piece, pairs):
        for owner, (left, right) in enumerate(pairs):
            put_square(owner, piece.offset, left, right)

    def produce_coeffs(index):
        return pieces_to_tiles(
            transposed_product(basis_all[:, index * block : (index + 1) * block], block_half[...]) * weight
        )

    def consume_coeffs(index):
        piece = coeffs[index]
        value = square_at(coeffs_tiles, piece.offset, block, half)
        window = slice(index * block, (index + 1) * block)
        change = matrix_product(operator[:, window], value)
        removed = matrix_product(basis_all[:, window], value)
        if index == 0:
            correction[...] = change
            residual[core] = block_half[...] - removed
        else:
            correction[...] += change
            residual[core] -= removed

    for piece in basis_gram:
        piece.out, piece.shared = basis_gram_tiles.at[core], True
    for piece in coeffs:
        piece.out, piece.shared = coeffs_tiles, False
    for piece in gram:
        piece.out, piece.shared = gram_tiles.at[core], True
    basis_gram[0].produce = lambda: upper_tiles(basis_product(first, first)) + upper_tiles(
        basis_product(second, second)
    )
    basis_gram[1].produce = lambda: pieces_to_tiles(basis_product(first, second))
    basis_gram[2].produce = lambda: pieces_to_tiles(basis_product(second, lax.rem(second + 1, 4)))
    basis_gram[3].produce = lambda: pieces_to_tiles(basis_product(core, core + 2))
    basis_gram[0].consume = consume_diagonals
    basis_gram[1].consume = lambda: consume_square(basis_gram[1], ((0, 1), (2, 3)))
    basis_gram[2].consume = lambda: consume_square(basis_gram[2], ((1, 2), (3, 0)))
    basis_gram[3].consume = lambda: consume_square(basis_gram[3], ((0, 2), (1, 3)))
    for index, piece in enumerate(coeffs):
        piece.produce = functools.partial(produce_coeffs, index)
        piece.consume = functools.partial(consume_coeffs, index)

    for copy in shared:
        copy.wait_recv()
    run([basis_gram[0:2], basis_gram[3:1:-1], coeffs[0:2], coeffs[2:4]])

    residual[core] -= matrix_product(basis_all[...], correction[...])
    swap = start(residual.at[core], residual.at[core], extra_send.at[2], extra_recv.at[2], partner)

    def produce_cross():
        swap.wait_recv()
        left = residual[0, :, lanes(core, half // 2)]
        return pieces_to_tiles(transposed_product(left, residual[1]) * weight)

    def consume_corners():
        gram_ref[...] = jnp.zeros_like(gram_ref)
        for owner in range(2):
            top, corner = upper_at(gram_tiles.at[owner], gram[0].offset, half)
            middle, base = half // 2, owner * half
            gram_ref[base : base + middle, base : base + half] = top
            gram_ref[base + middle : base + half, base + middle : base + half] = corner

    def consume_cross():
        middle = half // 2
        for owner in range(2):
            gram_ref[owner * middle : (owner + 1) * middle, half:] = square_at(
                gram_tiles.at[owner], gram[1].offset, middle, half
            )

    gram[0].produce = lambda: upper_tiles(transposed_product(residual[core], residual[core]) * weight)
    gram[0].consume = consume_corners
    gram[1].produce = produce_cross
    gram[1].consume = consume_cross
    run([gram])
    for owner in range(2):
        residual_ref[:, owner * half : (owner + 1) * half] = residual[owner, mine, :]
    for copy in sent:
        copy.wait_send()


def orthogonalize(basis, block, counts):
    slots, columns = basis.shape
    width = block.shape[1]
    row_size, grp_size = lax.axis_size("row"), lax.axis_size("grp")
    across, down = plane_sides(row_size // 2)
    sizes = {"x": across, "y": down, "z": grp_size}
    plan = make_plan(columns, width, sizes)
    basis_gram, coeffs, gram, place = plan
    weight = 1.0 / (slots * row_size * grp_size)
    half = width // 2
    vmem = pl.BlockSpec(memory_space=pltpu.VMEM)

    def tiles(*shape):
        return pltpu.VMEM(shape + (8, TILE), jnp.float32)

    def total(group):
        return sum(piece.tiles for piece in group)

    return pl.pallas_call(
        functools.partial(orthogonalize_kernel, plan, sizes, weight),
        out_shape=(
            jax.ShapeDtypeStruct((slots, width), jnp.float32),
            jax.ShapeDtypeStruct((width, width), jnp.float32),
        ),
        in_specs=[pl.BlockSpec(memory_space=pltpu.SMEM), vmem, vmem],
        out_specs=(vmem, vmem),
        scratch_shapes=[
            pltpu.VMEM((2 * slots, columns), jnp.float32),
            pltpu.VMEM((2 * slots, half), jnp.float32),
            pltpu.VMEM((slots, half), jnp.float32),
            tiles(place["source"]),
            tiles(place["held"]),
            tiles(place["partial"]),
            tiles(2, total(basis_gram)),
            tiles(total(coeffs)),
            tiles(2, total(gram)),
            pltpu.VMEM((columns, columns), jnp.float32),
            pltpu.VMEM((columns, half), jnp.float32),
            pltpu.VMEM((2, 2 * slots, half), jnp.float32),
            pltpu.SemaphoreType.DMA((place["copy"],)),
            pltpu.SemaphoreType.DMA((place["copy"],)),
            pltpu.SemaphoreType.DMA((3,)),
            pltpu.SemaphoreType.DMA((3,)),
        ],
        compiler_params=pltpu.CompilerParams(collective_id=0, has_side_effects=True),
        name="orthogonalize",
    )(counts, basis, block)


def eliminate(block):
    size = block.shape[0]
    count = size // 8
    sub = lax.broadcasted_iota(jnp.int32, (8, size), 0)
    lane = lax.broadcasted_iota(jnp.int32, (8, size), 1)
    left = [block[8 * b : 8 * b + 8] for b in range(count)]
    right = [(lane == sub + 8 * b).astype(jnp.float32) for b in range(count)]
    for j in range(size):
        home, inner = divmod(j, 8)
        row = left[home][inner : inner + 1]
        companion = right[home][inner : inner + 1]
        inverse = 1.0 / row[:, j : j + 1]
        row = row * inverse
        companion = companion * inverse
        for b in range(home, count):
            if b == home and inner == 7:
                continue
            factor = jnp.broadcast_to(left[b][:, j : j + 1], (8, size))
            if b == home:
                factor = jnp.where(sub > inner, factor, 0.0)
            left[b] = left[b] - factor * row
            right[b] = right[b] - factor * companion
    upper, inverted = [], []
    for b in range(count):
        diagonal = jnp.sum(jnp.where(lane == sub + 8 * b, left[b], 0.0), axis=1, keepdims=True)
        root = 1.0 / jnp.sqrt(diagonal)
        upper.append(jnp.where(lane >= sub + 8 * b, left[b] * root, 0.0))
        inverted.append(jnp.where(lane <= sub + 8 * b, right[b] * root, 0.0))
    return jnp.concatenate(upper, axis=0), jnp.concatenate(inverted, axis=0)


def factor_kernel(gram_ref, residual_ref, new_ref, factor_ref, work, rest):
    size = gram_ref.shape[0]
    work[...] = gram_ref[...]
    rest[...] = residual_ref[...]

    def step(index, carry):
        window = pl.ds(pl.multiple_of(index * TILE, TILE), TILE)
        upper, inverted = eliminate(work[window, window])
        panel = matrix_product(inverted, work[window, :])
        column = lax.broadcasted_iota(jnp.int32, (TILE, size), 1)
        panel = jnp.where(column >= (index + 1) * TILE, panel, 0.0)
        factor_ref[window, :] = panel
        factor_ref[window, window] = upper
        work[...] -= transposed_product(panel, panel)
        solved = lax.dot_general(
            rest[:, window],
            inverted,
            (((1,), (1,)), ((), ())),
            precision=HIGHEST,
            preferred_element_type=jnp.float32,
        )
        new_ref[:, window] = solved
        rest[...] -= matrix_product(solved, panel)
        return carry

    lax.fori_loop(0, size // TILE, step, 0)


def factor_and_solve(gram, residual):
    vmem = pl.BlockSpec(memory_space=pltpu.VMEM)
    return pl.pallas_call(
        factor_kernel,
        out_shape=(
            jax.ShapeDtypeStruct(residual.shape, jnp.float32),
            jax.ShapeDtypeStruct(gram.shape, jnp.float32),
        ),
        in_specs=[vmem, vmem],
        out_specs=(vmem, vmem),
        scratch_shapes=[pltpu.VMEM(gram.shape, jnp.float32), pltpu.VMEM(residual.shape, jnp.float32)],
        name="factor_and_solve",
    )(gram, residual)


def body(basis, block, counts):
    residual, gram = orthogonalize(basis, block, counts)
    return factor_and_solve(gram, residual)


def solution(mesh):
    placed = (P(("grp", "row"), None), P(("grp", "row"), None), P("grp", "row"))
    return jax.shard_map(
        body, mesh=mesh, in_specs=placed, out_specs=(P(("grp", "row"), None), P()), check_vma=False
    )
```

```python
import functools
import math

import jax
import jax.numpy as jnp
from jax import lax
from jax.experimental import pallas as pl
from jax.experimental.pallas import tpu as pltpu
from jax.sharding import PartitionSpec as P

HIGHEST = lax.Precision.HIGHEST
MESH = pl.DeviceIdType.MESH
TILE = 128


def transposed_product(left, right):
    return lax.dot_general(
        left,
        right,
        (((0,), (0,)), ((), ())),
        precision=HIGHEST,
        preferred_element_type=jnp.float32,
    )


def matrix_product(left, right):
    return jnp.dot(left, right, precision=HIGHEST, preferred_element_type=jnp.float32)


def plane_sides(chips):
    side = math.isqrt(chips)
    while chips % side:
        side -= 1
    return chips // side, side


class Piece:
    def __init__(self, tiles, order, chips):
        self.used = tiles
        self.tiles = -(-tiles // chips) * chips
        self.order = order


def make_plan(basis_columns, block_columns, sizes):
    chips = sizes["x"] * sizes["y"] * sizes["z"]
    block = basis_columns // 4
    half = block_columns // 2
    square = block * block // 1024
    corner = half * half // 1024
    forward, backward = ("x", "y", "z"), ("y", "x", "z")
    basis_gram = [
        Piece(2 * (square - square // 4), forward, chips),
        Piece(square, backward, chips),
        Piece(square, backward, chips),
        Piece(square, forward, chips),
    ]
    coeffs = [Piece(block * half // 1024, (forward, backward)[i % 2], chips) for i in range(4)]
    gram = [Piece(corner - corner // 4, forward, chips), Piece(corner // 2, backward, chips)]
    place = dict(copy=0, source=0, held=0, partial=0)
    for group in (basis_gram, coeffs, gram):
        offset = 0
        for piece in group:
            piece.offset = offset
            offset += piece.tiles
            piece.source = place["source"]
            place["source"] += piece.tiles
            piece.stages = []
            size = piece.tiles
            for axis in piece.order:
                count = sizes[axis]
                size //= count
                stage = dict(axis=axis, size=size, held=place["held"], partial=place["partial"])
                stage["scatter"] = place["copy"]
                stage["gather"] = place["copy"] + count - 1
                place["copy"] += 2 * (count - 1)
                place["held"] += (count - 1) * size
                place["partial"] += size
                piece.stages.append(stage)
            piece.partner = place["copy"]
            place["copy"] += 1
    return basis_gram, coeffs, gram, place


def pieces_to_tiles(value):
    rows, cols = value.shape
    return [value[:, i : i + TILE].reshape(rows // 8, 8, TILE) for i in range(0, cols, TILE)]


def orthogonalize_kernel(
    plan,
    sizes,
    weight,
    counts_ref,
    basis_ref,
    block_ref,
    residual_ref,
    gram_ref,
    basis_all,
    block_half,
    block_send,
    source,
    held,
    partial,
    basis_gram_tiles,
    coeffs_tiles,
    gram_tiles,
    operator,
    correction,
    residual,
    send_sem,
    recv_sem,
    extra_send,
    extra_recv,
):
    basis_gram, coeffs, gram, _ = plan
    slots = basis_ref.shape[0]
    columns = basis_ref.shape[1]
    half = block_ref.shape[1] // 2
    block = columns // 4

    row = lax.axis_index("row")
    core = lax.rem(row, 2)
    chip = lax.div(row, 2)
    me = {"x": lax.rem(chip, sizes["x"]), "y": lax.div(chip, sizes["x"]), "z": lax.axis_index("grp")}
    partner = {"row": row + 1 - 2 * core}

    def peer(axis, k):
        other = lax.rem(me[axis] + k, sizes[axis])
        if axis == "z":
            return {"grp": other}
        x, y = (other, me["y"]) if axis == "x" else (me["x"], other)
        return {"row": (y * sizes["x"] + x) * 2 + core}

    barrier = pltpu.get_barrier_semaphore()
    pl.semaphore_signal(barrier, inc=1, device_id=partner, device_id_type=MESH)
    for axis in sizes:
        for k in range(1, sizes[axis]):
            pl.semaphore_signal(barrier, inc=1, device_id=peer(axis, k), device_id_type=MESH)
    sent = []

    def start(source_ref, target_ref, sends, recvs, device):
        copy = pltpu.make_async_remote_copy(
            src_ref=source_ref,
            dst_ref=target_ref,
            send_sem=sends,
            recv_sem=recvs,
            device_id=device,
            device_id_type=MESH,
        )
        copy.start()
        sent.append(copy)
        return copy

    live = lax.broadcasted_iota(jnp.int32, (slots, 1), 0) < counts_ref[0, 0]
    mine = pl.ds(pl.multiple_of(core * slots, 8), slots)
    near = pl.ds(pl.multiple_of(core * half, TILE), half)
    far = pl.ds(pl.multiple_of((1 - core) * half, TILE), half)
    basis_all[mine, :] = jnp.where(live, basis_ref[...], 0.0)
    block_send[...] = jnp.where(live, block_ref[:, far], 0.0)
    block_half[mine, :] = jnp.where(live, block_ref[:, near], 0.0)
    pl.semaphore_wait(barrier, 1 + sum(size - 1 for size in sizes.values()))
    shared = [
        start(basis_all.at[mine], basis_all.at[mine], extra_send.at[0], extra_recv.at[0], partner),
        start(block_send, block_half.at[mine], extra_send.at[1], extra_recv.at[1], partner),
    ]

    def position(piece, depth):
        offset = 0
        for stage in piece.stages[:depth]:
            offset = offset + me[stage["axis"]] * stage["size"]
        return offset

    def scatter(piece, depth):
        stage = piece.stages[depth]
        axis, size = stage["axis"], stage["size"]
        if depth == 0:
            base, ref = piece.source, source
        else:
            base, ref = piece.stages[depth - 1]["partial"], partial
        piece.waiting = []
        for k in range(1, sizes[axis]):
            chunk = lax.rem(me[axis] + k, sizes[axis]) * size
            index = stage["scatter"] + k - 1
            piece.waiting.append(
                start(
                    ref.at[pl.ds(base + chunk, size)],
                    held.at[pl.ds(stage["held"] + (k - 1) * size, size)],
                    send_sem.at[index],
                    recv_sem.at[index],
                    peer(axis, k),
                )
            )

    def reduced(piece, depth):
        stage = piece.stages[depth]
        axis, size = stage["axis"], stage["size"]
        if depth == 0:
            base, ref = piece.source, source
        else:
            base, ref = piece.stages[depth - 1]["partial"], partial
        for copy in piece.waiting:
            copy.wait_recv()
        total = ref[pl.ds(base + me[axis] * size, size)]
        for k in range(sizes[axis] - 1):
            total = total + held[pl.ds(stage["held"] + k * size, size)]
        return total

    def gather(piece, depth):
        stage = piece.stages[depth]
        axis = stage["axis"]
        place = piece.out.at[pl.ds(piece.offset + position(piece, depth + 1), stage["size"])]
        piece.waiting = []
        for k in range(1, sizes[axis]):
            index = stage["gather"] + k - 1
            piece.waiting.append(start(place, place, send_sem.at[index], recv_sem.at[index], peer(axis, k)))

    def advance(piece, step):
        if step == 0:
            blocks = piece.produce()
            offset = piece.source
            for value in blocks:
                source[pl.ds(offset, value.shape[0])] = value
                offset += value.shape[0]
            if piece.used < piece.tiles:
                source[pl.ds(offset, piece.tiles - piece.used)] = jnp.zeros(
                    (piece.tiles - piece.used, 8, TILE), jnp.float32
                )
            scatter(piece, 0)
        elif step < 3:
            stage = piece.stages[step - 1]
            partial[pl.ds(stage["partial"], stage["size"])] = reduced(piece, step - 1)
            scatter(piece, step)
        elif step == 3:
            size = piece.stages[2]["size"]
            piece.out[pl.ds(piece.offset + position(piece, 3), size)] = reduced(piece, 2)
            gather(piece, 2)
        elif step < 6:
            for copy in piece.waiting:
                copy.wait_recv()
            gather(piece, 5 - step)
        elif step == 6:
            for copy in piece.waiting:
                copy.wait_recv()
            if piece.shared:
                place = piece.out.at[pl.ds(piece.offset, piece.tiles)]
                index = piece.partner
                piece.waiting = [start(place, place, send_sem.at[index], recv_sem.at[index], partner)]
            else:
                piece.consume()
        elif step == 7 and piece.shared:
            for copy in piece.waiting:
                copy.wait_recv()
            piece.consume()

    def run(pairs):
        for tick in range(len(pairs) + 7):
            for index, pair in enumerate(pairs):
                if 0 <= tick - index <= 7:
                    for piece in pair:
                        advance(piece, tick - index)

    def lanes(index, width):
        return pl.ds(pl.multiple_of(index * width, TILE), width)

    first, second = 2 * core, 2 * core + 1

    def basis_product(left, right):
        return transposed_product(basis_all[:, lanes(left, block)], basis_all[:, lanes(right, block)]) * weight

    def upper_tiles(value):
        middle = value.shape[0] // 2
        return pieces_to_tiles(value[:middle]) + pieces_to_tiles(value[middle:, middle:])

    def square_at(ref, offset, rows, cols):
        parts = [
            ref[pl.ds(offset + i * (rows // 8), rows // 8)].reshape(rows, TILE) for i in range(cols // TILE)
        ]
        return jnp.concatenate(parts, axis=1)

    def upper_at(ref, offset, size):
        middle = size // 2
        top = square_at(ref, offset, middle, size)
        corner = square_at(ref, offset + middle * size // 1024, middle, middle)
        return top, corner

    square = block * block // 1024

    def put_diagonal(owner, offset, index):
        top, corner = upper_at(basis_gram_tiles.at[owner], offset, block)
        middle = block // 2
        whole = jnp.concatenate([top, jnp.concatenate([top[:, middle:].T, corner], axis=1)], axis=0)
        unit = lax.broadcasted_iota(jnp.int32, whole.shape, 0) == lax.broadcasted_iota(jnp.int32, whole.shape, 1)
        window = slice(index * block, (index + 1) * block)
        operator[window, window] = jnp.where(unit, 1.0, 0.0) - whole

    def put_square(owner, offset, left, right):
        whole = -square_at(basis_gram_tiles.at[owner], offset, block, block)
        rows, cols = slice(left * block, (left + 1) * block), slice(right * block, (right + 1) * block)
        operator[rows, cols] = whole
        operator[cols, rows] = whole.T

    def consume_diagonals():
        offset = basis_gram[0].offset
        for owner in range(2):
            put_diagonal(owner, offset, 2 * owner)
            put_diagonal(owner, offset + square - square // 4, 2 * owner + 1)

    def consume_square(piece, pairs):
        for owner, (left, right) in enumerate(pairs):
            put_square(owner, piece.offset, left, right)

    def produce_coeffs(index):
        return pieces_to_tiles(
            transposed_product(basis_all[:, index * block : (index + 1) * block], block_half[...]) * weight
        )

    def consume_coeffs(index):
        piece = coeffs[index]
        value = square_at(coeffs_tiles, piece.offset, block, half)
        window = slice(index * block, (index + 1) * block)
        change = matrix_product(operator[:, window], value)
        removed = matrix_product(basis_all[:, window], value)
        if index == 0:
            correction[...] = change
            residual[core] = block_half[...] - removed
        else:
            correction[...] += change
            residual[core] -= removed

    for piece in basis_gram:
        piece.out, piece.shared = basis_gram_tiles.at[core], True
    for piece in coeffs:
        piece.out, piece.shared = coeffs_tiles, False
    for piece in gram:
        piece.out, piece.shared = gram_tiles.at[core], True
    basis_gram[0].produce = lambda: upper_tiles(basis_product(first, first)) + upper_tiles(
        basis_product(second, second)
    )
    basis_gram[1].produce = lambda: pieces_to_tiles(basis_product(first, second))
    basis_gram[2].produce = lambda: pieces_to_tiles(basis_product(second, lax.rem(second + 1, 4)))
    basis_gram[3].produce = lambda: pieces_to_tiles(basis_product(core, core + 2))
    basis_gram[0].consume = consume_diagonals
    basis_gram[1].consume = lambda: consume_square(basis_gram[1], ((0, 1), (2, 3)))
    basis_gram[2].consume = lambda: consume_square(basis_gram[2], ((1, 2), (3, 0)))
    basis_gram[3].consume = lambda: consume_square(basis_gram[3], ((0, 2), (1, 3)))
    for index, piece in enumerate(coeffs):
        piece.produce = functools.partial(produce_coeffs, index)
        piece.consume = functools.partial(consume_coeffs, index)

    for copy in shared:
        copy.wait_recv()
    run([basis_gram[0:2], basis_gram[3:1:-1], coeffs[0:2], coeffs[2:4]])

    residual[core] -= matrix_product(basis_all[...], correction[...])
    swap = start(residual.at[core], residual.at[core], extra_send.at[2], extra_recv.at[2], partner)

    def produce_cross():
        swap.wait_recv()
        left = residual[0, :, lanes(core, half // 2)]
        return pieces_to_tiles(transposed_product(left, residual[1]) * weight)

    def consume_corners():
        gram_ref[...] = jnp.zeros_like(gram_ref)
        for owner in range(2):
            top, corner = upper_at(gram_tiles.at[owner], gram[0].offset, half)
            middle, base = half // 2, owner * half
            gram_ref[base : base + middle, base : base + half] = top
            gram_ref[base + middle : base + half, base + middle : base + half] = corner

    def consume_cross():
        middle = half // 2
        for owner in range(2):
            gram_ref[owner * middle : (owner + 1) * middle, half:] = square_at(
                gram_tiles.at[owner], gram[1].offset, middle, half
            )

    gram[0].produce = lambda: upper_tiles(transposed_product(residual[core], residual[core]) * weight)
    gram[0].consume = consume_corners
    gram[1].produce = produce_cross
    gram[1].consume = consume_cross
    run([gram])
    for owner in range(2):
        residual_ref[:, owner * half : (owner + 1) * half] = residual[owner, mine, :]
    for copy in sent:
        copy.wait_send()


def orthogonalize(basis, block, counts):
    slots, columns = basis.shape
    width = block.shape[1]
    row_size, grp_size = lax.axis_size("row"), lax.axis_size("grp")
    across, down = plane_sides(row_size // 2)
    sizes = {"x": across, "y": down, "z": grp_size}
    plan = make_plan(columns, width, sizes)
    basis_gram, coeffs, gram, place = plan
    weight = 1.0 / (slots * row_size * grp_size)
    half = width // 2
    vmem = pl.BlockSpec(memory_space=pltpu.VMEM)

    def tiles(*shape):
        return pltpu.VMEM(shape + (8, TILE), jnp.float32)

    def total(group):
        return sum(piece.tiles for piece in group)

    return pl.pallas_call(
        functools.partial(orthogonalize_kernel, plan, sizes, weight),
        out_shape=(
            jax.ShapeDtypeStruct((slots, width), jnp.float32),
            jax.ShapeDtypeStruct((width, width), jnp.float32),
        ),
        in_specs=[pl.BlockSpec(memory_space=pltpu.SMEM), vmem, vmem],
        out_specs=(vmem, vmem),
        scratch_shapes=[
            pltpu.VMEM((2 * slots, columns), jnp.float32),
            pltpu.VMEM((2 * slots, half), jnp.float32),
            pltpu.VMEM((slots, half), jnp.float32),
            tiles(place["source"]),
            tiles(place["held"]),
            tiles(place["partial"]),
            tiles(2, total(basis_gram)),
            tiles(total(coeffs)),
            tiles(2, total(gram)),
            pltpu.VMEM((columns, columns), jnp.float32),
            pltpu.VMEM((columns, half), jnp.float32),
            pltpu.VMEM((2, 2 * slots, half), jnp.float32),
            pltpu.SemaphoreType.DMA((place["copy"],)),
            pltpu.SemaphoreType.DMA((place["copy"],)),
            pltpu.SemaphoreType.DMA((3,)),
            pltpu.SemaphoreType.DMA((3,)),
        ],
        compiler_params=pltpu.CompilerParams(collective_id=0, has_side_effects=True),
        name="orthogonalize",
    )(counts, basis, block)


BLOCK = 64
GROUP = 8


def eliminate(square):
    size = square.shape[0]
    count = size // GROUP
    shape = (GROUP, 2 * size)
    sub = lax.broadcasted_iota(jnp.int32, shape, 0)
    lane = lax.broadcasted_iota(jnp.int32, shape, 1)
    wide = [
        jnp.concatenate(
            [
                square[GROUP * b : GROUP * (b + 1)],
                (lane[:, :size] == sub[:, :size] + GROUP * b).astype(jnp.float32),
            ],
            axis=1,
        )
        for b in range(count)
    ]

    def across(value, index):
        return jnp.broadcast_to(value[:, index : index + 1], shape)

    def down(value, index):
        return jnp.broadcast_to(value[index : index + 1], shape)

    roots = []
    for g in range(count):
        columns = {b: [across(wide[b], GROUP * g + i) for i in range(GROUP)] for b in range(g, count)}
        root = jnp.zeros(shape, jnp.float32)
        for i in range(GROUP):
            pivot = down(columns[g][i], i)
            inverse = 1.0 / pivot
            root = jnp.where(sub == i, 1.0 / jnp.sqrt(pivot), root)
            later = [down(columns[g][j], i) for j in range(i + 1, GROUP)]
            row = down(wide[g], i)
            for b in range(g, count):
                factor = columns[b][i] * inverse
                if b == g:
                    if i == GROUP - 1:
                        continue
                    factor = jnp.where(sub > i, factor, 0.0)
                for j in range(i + 1, GROUP):
                    columns[b][j] = columns[b][j] - factor * later[j - i - 1]
                wide[b] = wide[b] - factor * row
        roots.append(root)
    upper, inverted = [], []
    for b in range(count):
        value = wide[b] * roots[b]
        upper.append(jnp.where((lane >= sub + GROUP * b)[:, :size], value[:, :size], 0.0))
        inverted.append(jnp.where((lane <= sub + GROUP * b)[:, :size], value[:, size:], 0.0))
    return jnp.concatenate(upper, axis=0), jnp.concatenate(inverted, axis=0)


def factor_kernel(gram_ref, residual_ref, new_ref, factor_ref, work, rest):
    size = gram_ref.shape[0]
    steps = size // BLOCK
    work[...] = gram_ref[...]
    rest[...] = residual_ref[...]
    square = work[:BLOCK, :BLOCK]
    for step in range(steps):
        here, after, beyond = (BLOCK * (step + i) for i in range(3))
        upper, inverted = eliminate(square)
        if step:
            factor_ref[here:after, :here] = jnp.zeros((BLOCK, here), jnp.float32)
        factor_ref[here:after, here:after] = upper
        if after < size:
            near = matrix_product(inverted, work[here:after, after:beyond])
            square = work[after:beyond, after:beyond] - transposed_product(near, near)
            factor_ref[here:after, after:beyond] = near
            if beyond < size:
                panel = matrix_product(inverted, work[here:after, beyond:])
                factor_ref[here:after, beyond:] = panel
                work[after:beyond, beyond:] -= transposed_product(near, panel)
                work[beyond:, beyond:] -= transposed_product(panel, panel)
        solved = lax.dot_general(
            rest[:, here:after],
            inverted,
            (((1,), (1,)), ((), ())),
            precision=HIGHEST,
            preferred_element_type=jnp.float32,
        )
        new_ref[:, here:after] = solved
        if after < size:
            rest[:, after:] -= matrix_product(solved, factor_ref[here:after, after:])


def factor_and_solve(gram, residual):
    vmem = pl.BlockSpec(memory_space=pltpu.VMEM)
    return pl.pallas_call(
        factor_kernel,
        out_shape=(
            jax.ShapeDtypeStruct(residual.shape, jnp.float32),
            jax.ShapeDtypeStruct(gram.shape, jnp.float32),
        ),
        in_specs=[vmem, vmem],
        out_specs=(vmem, vmem),
        scratch_shapes=[pltpu.VMEM(gram.shape, jnp.float32), pltpu.VMEM(residual.shape, jnp.float32)],
        name="factor_and_solve",
    )(gram, residual)


def body(basis, block, counts):
    residual, gram = orthogonalize(basis, block, counts)
    return factor_and_solve(gram, residual)


def solution(mesh):
    placed = (P(("grp", "row"), None), P(("grp", "row"), None), P("grp", "row"))
    return jax.shard_map(
        body, mesh=mesh, in_specs=placed, out_specs=(P(("grp", "row"), None), P()), check_vma=False
    )
```

```python
import functools
import math

import jax
import jax.numpy as jnp
from jax import lax
from jax.experimental import pallas as pl
from jax.experimental.pallas import tpu as pltpu
from jax.sharding import PartitionSpec as P

HIGHEST = lax.Precision.HIGHEST
MESH = pl.DeviceIdType.MESH
TILE = 128


def transposed_product(left, right):
    return lax.dot_general(
        left,
        right,
        (((0,), (0,)), ((), ())),
        precision=HIGHEST,
        preferred_element_type=jnp.float32,
    )


def matrix_product(left, right):
    return jnp.dot(left, right, precision=HIGHEST, preferred_element_type=jnp.float32)


AXES = {"x": "x", "y": "y", "z": "z", "n": "near", "f": "far", "p": "plane"}
FIRST_ROUTES = ("xyz", "yxz", "zxy", "yxz", "xyz", "yxz", "yxz", "xyz")
FIRST_ORDER = (0, 1, 2, 3, 1, 0, 4, 5, 3, 2, 1, 0, 6, 7, 5, 4, 3, 2, 1, 0, 7, 6, 5, 4, 3, 2, 1, 0, 7, 6, 5, 4, 3, 2, 1, 0, 7, 6, 5, 4, 3, 2, 1, 0, 7, 6, 5, 4, 3, 2, 1, 0, -1, -2, 7, 6, 5, 4, 3, 2, -3, -4, -5, -6, 7, 6, -7, -8)
SECOND_ROUTES = ("pz", "zp")
SECOND_ORDER = (0, 1, 0, 1, 0, 1, 1, 0, 0, 1, 0, -1, 1, -2)


def plane_sides(chips):
    side = math.isqrt(chips)
    while chips % side:
        side -= 1
    return chips // side, side


class Piece:
    def __init__(self, tiles, order, chips):
        self.used = tiles
        self.tiles = -(-tiles // chips) * chips
        self.order = order
        self.step = 0


def make_plan(basis_columns, block_columns, sizes):
    chips = sizes["plane"] * sizes["z"]
    block = basis_columns // 4
    half = block_columns // 2
    square = block * block // 1024
    corner = half * half // 1024
    diagonal, corner = square - square // 4, corner - corner // 4
    shapes = [2 * diagonal, square, square, square] + [block * half // 1024] * 4
    first = [Piece(tiles, [AXES[letter] for letter in route], chips) for tiles, route in zip(shapes, FIRST_ROUTES)]
    second = [Piece(tiles, [AXES[letter] for letter in route], chips) for tiles, route in zip((corner, half * half // 2048), SECOND_ROUTES)]
    basis_gram, coeffs, gram = first[:4], first[4:], second
    place = dict(copy=0, source=0, held=0, partial=0)
    for group in (basis_gram, coeffs, gram):
        offset = 0
        for piece in group:
            piece.offset = offset
            offset += piece.tiles
            piece.source = place["source"]
            place["source"] += piece.tiles
            piece.stages = []
            size = piece.tiles
            for axis in piece.order:
                count = sizes[axis]
                size //= count
                stage = dict(axis=axis, size=size, held=place["held"], partial=place["partial"])
                stage["scatter"] = place["copy"]
                stage["gather"] = place["copy"] + count - 1
                place["copy"] += 2 * (count - 1)
                place["held"] += (count - 1) * size
                place["partial"] += size
                piece.stages.append(stage)
            piece.partner = place["copy"]
            place["copy"] += 1
    return basis_gram, coeffs, gram, place


def pieces_to_tiles(value):
    rows, cols = value.shape
    return [value[:, i : i + TILE].reshape(rows // 8, 8, TILE) for i in range(0, cols, TILE)]


def orthogonalize_kernel(
    plan,
    sizes,
    weight,
    counts_ref,
    basis_ref,
    block_ref,
    residual_ref,
    gram_ref,
    basis_all,
    block_half,
    block_send,
    source,
    held,
    partial,
    basis_gram_tiles,
    coeffs_tiles,
    gram_tiles,
    operator,
    correction,
    residual,
    send_sem,
    recv_sem,
    extra_send,
    extra_recv,
):
    basis_gram, coeffs, gram, _ = plan
    slots = basis_ref.shape[0]
    columns = basis_ref.shape[1]
    half = block_ref.shape[1] // 2
    block = columns // 4

    row = lax.axis_index("row")
    core = lax.rem(row, 2)
    chip = lax.div(row, 2)
    me = {
        "x": lax.rem(chip, sizes["x"]),
        "y": lax.div(chip, sizes["x"]),
        "z": lax.axis_index("grp"),
        "plane": chip,
        "near": lax.rem(lax.axis_index("grp"), sizes["near"]),
        "far": lax.div(lax.axis_index("grp"), sizes["near"]),
    }
    partner = {"row": row + 1 - 2 * core}

    def peer(axis, k):
        other = lax.rem(me[axis] + k, sizes[axis])
        if axis == "z":
            return {"grp": other}
        if axis == "near":
            return {"grp": me["far"] * sizes["near"] + other}
        if axis == "far":
            return {"grp": other * sizes["near"] + me["near"]}
        if axis == "plane":
            return {"row": other * 2 + core}
        x, y = (other, me["y"]) if axis == "x" else (me["x"], other)
        return {"row": (y * sizes["x"] + x) * 2 + core}

    barrier = pltpu.get_barrier_semaphore()
    pl.semaphore_signal(barrier, inc=1, device_id=partner, device_id_type=MESH)
    for axis in ("plane", "z"):
        for k in range(1, sizes[axis]):
            pl.semaphore_signal(barrier, inc=1, device_id=peer(axis, k), device_id_type=MESH)
    sent = []

    def start(source_ref, target_ref, sends, recvs, device):
        copy = pltpu.make_async_remote_copy(
            src_ref=source_ref,
            dst_ref=target_ref,
            send_sem=sends,
            recv_sem=recvs,
            device_id=device,
            device_id_type=MESH,
        )
        copy.start()
        sent.append(copy)
        return copy

    live = lax.broadcasted_iota(jnp.int32, (slots, 1), 0) < counts_ref[0, 0]
    mine = pl.ds(pl.multiple_of(core * slots, 8), slots)
    near = pl.ds(pl.multiple_of(core * half, TILE), half)
    far = pl.ds(pl.multiple_of((1 - core) * half, TILE), half)
    basis_all[mine, :] = jnp.where(live, basis_ref[...], 0.0)
    block_send[...] = jnp.where(live, block_ref[:, far], 0.0)
    block_half[mine, :] = jnp.where(live, block_ref[:, near], 0.0)
    pl.semaphore_wait(barrier, sizes["plane"] + sizes["z"] - 1)
    shared = [
        start(basis_all.at[mine], basis_all.at[mine], extra_send.at[0], extra_recv.at[0], partner),
        start(block_send, block_half.at[mine], extra_send.at[1], extra_recv.at[1], partner),
    ]

    def position(piece, depth):
        offset = 0
        for stage in piece.stages[:depth]:
            offset = offset + me[stage["axis"]] * stage["size"]
        return offset

    def scatter(piece, depth):
        stage = piece.stages[depth]
        axis, size = stage["axis"], stage["size"]
        if depth == 0:
            base, ref = piece.source, source
        else:
            base, ref = piece.stages[depth - 1]["partial"], partial
        piece.waiting = []
        for k in range(1, sizes[axis]):
            chunk = lax.rem(me[axis] + k, sizes[axis]) * size
            index = stage["scatter"] + k - 1
            piece.waiting.append(
                start(
                    ref.at[pl.ds(base + chunk, size)],
                    held.at[pl.ds(stage["held"] + (k - 1) * size, size)],
                    send_sem.at[index],
                    recv_sem.at[index],
                    peer(axis, k),
                )
            )

    def reduced(piece, depth):
        stage = piece.stages[depth]
        axis, size = stage["axis"], stage["size"]
        if depth == 0:
            base, ref = piece.source, source
        else:
            base, ref = piece.stages[depth - 1]["partial"], partial
        for copy in piece.waiting:
            copy.wait_recv()
        total = ref[pl.ds(base + me[axis] * size, size)]
        for k in range(sizes[axis] - 1):
            total = total + held[pl.ds(stage["held"] + k * size, size)]
        return total

    def gather(piece, depth):
        stage = piece.stages[depth]
        axis = stage["axis"]
        place = piece.out.at[pl.ds(piece.offset + position(piece, depth + 1), stage["size"])]
        piece.waiting = []
        for k in range(1, sizes[axis]):
            index = stage["gather"] + k - 1
            piece.waiting.append(start(place, place, send_sem.at[index], recv_sem.at[index], peer(axis, k)))

    def stage_source(piece):
        offset = piece.source
        for value in piece.produce():
            source[pl.ds(offset, value.shape[0])] = value
            offset += value.shape[0]
        if piece.used < piece.tiles:
            source[pl.ds(offset, piece.tiles - piece.used)] = jnp.zeros(
                (piece.tiles - piece.used, 8, TILE), jnp.float32
            )

    def advance(piece):
        depth = len(piece.stages)
        step = piece.step
        piece.step += 1
        if step == 0:
            stage_source(piece)
            scatter(piece, 0)
            return
        if step < depth:
            stage = piece.stages[step - 1]
            partial[pl.ds(stage["partial"], stage["size"])] = reduced(piece, step - 1)
            scatter(piece, step)
            return
        if step == depth:
            size = piece.stages[-1]["size"]
            piece.out[pl.ds(piece.offset + position(piece, depth), size)] = reduced(piece, depth - 1)
            gather(piece, depth - 1)
            return
        for copy in piece.waiting:
            copy.wait_recv()
        piece.waiting = []
        if step < 2 * depth:
            gather(piece, 2 * depth - 1 - step)
        elif step == 2 * depth and piece.shared:
            place = piece.out.at[pl.ds(piece.offset, piece.tiles)]
            index = piece.partner
            piece.waiting = [start(place, place, send_sem.at[index], recv_sem.at[index], partner)]

    def run(pieces, order):
        for entry in order:
            if entry < 0:
                pieces[~entry].consume()
            else:
                advance(pieces[entry])

    def lanes(index, width):
        return pl.ds(pl.multiple_of(index * width, TILE), width)

    first, second = 2 * core, 2 * core + 1

    def basis_product(left, right):
        return transposed_product(basis_all[:, lanes(left, block)], basis_all[:, lanes(right, block)]) * weight

    def upper_tiles(value):
        middle = value.shape[0] // 2
        return pieces_to_tiles(value[:middle]) + pieces_to_tiles(value[middle:, middle:])

    def square_at(ref, offset, rows, cols):
        parts = [
            ref[pl.ds(offset + i * (rows // 8), rows // 8)].reshape(rows, TILE) for i in range(cols // TILE)
        ]
        return jnp.concatenate(parts, axis=1)

    def upper_at(ref, offset, size):
        middle = size // 2
        top = square_at(ref, offset, middle, size)
        corner = square_at(ref, offset + middle * size // 1024, middle, middle)
        return top, corner

    square = block * block // 1024

    def put_diagonal(owner, offset, index):
        top, corner = upper_at(basis_gram_tiles.at[owner], offset, block)
        middle = block // 2
        whole = jnp.concatenate([top, jnp.concatenate([top[:, middle:].T, corner], axis=1)], axis=0)
        unit = lax.broadcasted_iota(jnp.int32, whole.shape, 0) == lax.broadcasted_iota(jnp.int32, whole.shape, 1)
        window = slice(index * block, (index + 1) * block)
        operator[window, window] = jnp.where(unit, 1.0, 0.0) - whole

    def put_square(owner, offset, left, right):
        whole = -square_at(basis_gram_tiles.at[owner], offset, block, block)
        rows, cols = slice(left * block, (left + 1) * block), slice(right * block, (right + 1) * block)
        operator[rows, cols] = whole
        operator[cols, rows] = whole.T

    def consume_diagonals():
        offset = basis_gram[0].offset
        for owner in range(2):
            put_diagonal(owner, offset, 2 * owner)
            put_diagonal(owner, offset + square - square // 4, 2 * owner + 1)

    def consume_square(piece, pairs):
        for owner, (left, right) in enumerate(pairs):
            put_square(owner, piece.offset, left, right)

    def produce_coeffs(index):
        return pieces_to_tiles(
            transposed_product(basis_all[:, index * block : (index + 1) * block], block_half[...]) * weight
        )

    def consume_coeffs(index):
        piece = coeffs[index]
        value = square_at(coeffs_tiles, piece.offset, block, half)
        window = slice(index * block, (index + 1) * block)
        change = matrix_product(operator[:, window], value)
        removed = matrix_product(basis_all[:, window], value)
        if index == 0:
            correction[...] = change
            residual[core] = block_half[...] - removed
        else:
            correction[...] += change
            residual[core] -= removed

    for piece in basis_gram:
        piece.out, piece.shared = basis_gram_tiles.at[core], True
    for piece in coeffs:
        piece.out, piece.shared = coeffs_tiles, False
    for piece in gram:
        piece.out, piece.shared = gram_tiles.at[core], True
    basis_gram[0].produce = lambda: upper_tiles(basis_product(first, first)) + upper_tiles(
        basis_product(second, second)
    )
    basis_gram[1].produce = lambda: pieces_to_tiles(basis_product(first, second))
    basis_gram[2].produce = lambda: pieces_to_tiles(basis_product(second, lax.rem(second + 1, 4)))
    basis_gram[3].produce = lambda: pieces_to_tiles(basis_product(core, core + 2))
    basis_gram[0].consume = consume_diagonals
    basis_gram[1].consume = lambda: consume_square(basis_gram[1], ((0, 1), (2, 3)))
    basis_gram[2].consume = lambda: consume_square(basis_gram[2], ((1, 2), (3, 0)))
    basis_gram[3].consume = lambda: consume_square(basis_gram[3], ((0, 2), (1, 3)))
    for index, piece in enumerate(coeffs):
        piece.produce = functools.partial(produce_coeffs, index)
        piece.consume = functools.partial(consume_coeffs, index)

    for copy in shared:
        copy.wait_recv()
    run(basis_gram + coeffs, FIRST_ORDER)

    residual[core] -= matrix_product(basis_all[...], correction[...])
    swap = start(residual.at[core], residual.at[core], extra_send.at[2], extra_recv.at[2], partner)

    gram_ref[...] = jnp.zeros_like(gram_ref)

    def produce_cross():
        swap.wait_recv()
        left = residual[0, :, lanes(core, half // 2)]
        return pieces_to_tiles(transposed_product(left, residual[1]) * weight)

    def consume_corners():
        for owner in range(2):
            top, corner = upper_at(gram_tiles.at[owner], gram[0].offset, half)
            middle, base = half // 2, owner * half
            gram_ref[base : base + middle, base : base + half] = top
            gram_ref[base + middle : base + half, base + middle : base + half] = corner

    def consume_cross():
        middle = half // 2
        for owner in range(2):
            gram_ref[owner * middle : (owner + 1) * middle, half:] = square_at(
                gram_tiles.at[owner], gram[1].offset, middle, half
            )

    gram[0].produce = lambda: upper_tiles(transposed_product(residual[core], residual[core]) * weight)
    gram[0].consume = consume_corners
    gram[1].produce = produce_cross
    gram[1].consume = consume_cross
    run(gram, SECOND_ORDER)
    for owner in range(2):
        residual_ref[:, owner * half : (owner + 1) * half] = residual[owner, mine, :]
    for copy in sent:
        copy.wait_send()


def orthogonalize(basis, block, counts):
    slots, columns = basis.shape
    width = block.shape[1]
    row_size, grp_size = lax.axis_size("row"), lax.axis_size("grp")
    across, down = plane_sides(row_size // 2)
    near = 2 - grp_size % 2
    sizes = {"x": across, "y": down, "z": grp_size, "plane": across * down, "near": near, "far": grp_size // near}
    plan = make_plan(columns, width, sizes)
    basis_gram, coeffs, gram, place = plan
    weight = 1.0 / (slots * row_size * grp_size)
    half = width // 2
    vmem = pl.BlockSpec(memory_space=pltpu.VMEM)

    def tiles(*shape):
        return pltpu.VMEM(shape + (8, TILE), jnp.float32)

    def total(group):
        return sum(piece.tiles for piece in group)

    return pl.pallas_call(
        functools.partial(orthogonalize_kernel, plan, sizes, weight),
        out_shape=(
            jax.ShapeDtypeStruct((slots, width), jnp.float32),
            jax.ShapeDtypeStruct((width, width), jnp.float32),
        ),
        in_specs=[pl.BlockSpec(memory_space=pltpu.SMEM), vmem, vmem],
        out_specs=(vmem, vmem),
        scratch_shapes=[
            pltpu.VMEM((2 * slots, columns), jnp.float32),
            pltpu.VMEM((2 * slots, half), jnp.float32),
            pltpu.VMEM((slots, half), jnp.float32),
            tiles(place["source"]),
            tiles(place["held"]),
            tiles(place["partial"]),
            tiles(2, total(basis_gram)),
            tiles(total(coeffs)),
            tiles(2, total(gram)),
            pltpu.VMEM((columns, columns), jnp.float32),
            pltpu.VMEM((columns, half), jnp.float32),
            pltpu.VMEM((2, 2 * slots, half), jnp.float32),
            pltpu.SemaphoreType.DMA((place["copy"],)),
            pltpu.SemaphoreType.DMA((place["copy"],)),
            pltpu.SemaphoreType.DMA((3,)),
            pltpu.SemaphoreType.DMA((3,)),
        ],
        compiler_params=pltpu.CompilerParams(collective_id=0, has_side_effects=True),
        name="orthogonalize",
    )(counts, basis, block)


BLOCK = 64
GROUP = 8


def eliminate(square):
    size = square.shape[0]
    count = size // GROUP
    shape = (GROUP, 2 * size)
    sub = lax.broadcasted_iota(jnp.int32, shape, 0)
    lane = lax.broadcasted_iota(jnp.int32, shape, 1)
    wide = [
        jnp.concatenate(
            [
                square[GROUP * b : GROUP * (b + 1)],
                (lane[:, :size] == sub[:, :size] + GROUP * b).astype(jnp.float32),
            ],
            axis=1,
        )
        for b in range(count)
    ]

    def across(value, index):
        return jnp.broadcast_to(value[:, index : index + 1], shape)

    def down(value, index):
        return jnp.broadcast_to(value[index : index + 1], shape)

    roots = []
    for g in range(count):
        columns = {b: [across(wide[b], GROUP * g + i) for i in range(GROUP)] for b in range(g, count)}
        root = jnp.zeros(shape, jnp.float32)
        for i in range(GROUP):
            pivot = down(columns[g][i], i)
            inverse = 1.0 / pivot
            root = jnp.where(sub == i, 1.0 / jnp.sqrt(pivot), root)
            later = [down(columns[g][j], i) for j in range(i + 1, GROUP)]
            row = down(wide[g], i)
            for b in range(g, count):
                factor = columns[b][i] * inverse
                if b == g:
                    if i == GROUP - 1:
                        continue
                    factor = jnp.where(sub > i, factor, 0.0)
                for j in range(i + 1, GROUP):
                    columns[b][j] = columns[b][j] - factor * later[j - i - 1]
                wide[b] = wide[b] - factor * row
        roots.append(root)
    upper, inverted = [], []
    for b in range(count):
        value = wide[b] * roots[b]
        upper.append(jnp.where((lane >= sub + GROUP * b)[:, :size], value[:, :size], 0.0))
        inverted.append(jnp.where((lane <= sub + GROUP * b)[:, :size], value[:, size:], 0.0))
    return jnp.concatenate(upper, axis=0), jnp.concatenate(inverted, axis=0)


def factor_kernel(gram_ref, residual_ref, new_ref, factor_ref, work, rest):
    size = gram_ref.shape[0]
    steps = size // BLOCK
    work[...] = gram_ref[...]
    rest[...] = residual_ref[...]
    square = work[:BLOCK, :BLOCK]
    for step in range(steps):
        here, after, beyond = (BLOCK * (step + i) for i in range(3))
        upper, inverted = eliminate(square)
        if step:
            factor_ref[here:after, :here] = jnp.zeros((BLOCK, here), jnp.float32)
        factor_ref[here:after, here:after] = upper
        if after < size:
            near = matrix_product(inverted, work[here:after, after:beyond])
            square = work[after:beyond, after:beyond] - transposed_product(near, near)
            factor_ref[here:after, after:beyond] = near
            if beyond < size:
                panel = matrix_product(inverted, work[here:after, beyond:])
                factor_ref[here:after, beyond:] = panel
                work[after:beyond, beyond:] -= transposed_product(near, panel)
                work[beyond:, beyond:] -= transposed_product(panel, panel)
        solved = lax.dot_general(
            rest[:, here:after],
            inverted,
            (((1,), (1,)), ((), ())),
            precision=HIGHEST,
            preferred_element_type=jnp.float32,
        )
        new_ref[:, here:after] = solved
        if after < size:
            rest[:, after:] -= matrix_product(solved, factor_ref[here:after, after:])


def factor_and_solve(gram, residual):
    vmem = pl.BlockSpec(memory_space=pltpu.VMEM)
    return pl.pallas_call(
        factor_kernel,
        out_shape=(
            jax.ShapeDtypeStruct(residual.shape, jnp.float32),
            jax.ShapeDtypeStruct(gram.shape, jnp.float32),
        ),
        in_specs=[vmem, vmem],
        out_specs=(vmem, vmem),
        scratch_shapes=[pltpu.VMEM(gram.shape, jnp.float32), pltpu.VMEM(residual.shape, jnp.float32)],
        name="factor_and_solve",
    )(gram, residual)


def body(basis, block, counts):
    residual, gram = orthogonalize(basis, block, counts)
    return factor_and_solve(gram, residual)


def solution(mesh):
    placed = (P(("grp", "row"), None), P(("grp", "row"), None), P("grp", "row"))
    return jax.shard_map(
        body, mesh=mesh, in_specs=placed, out_specs=(P(("grp", "row"), None), P()), check_vma=False
    )
```

```python
import functools
import math

import jax
import jax.numpy as jnp
from jax import lax
from jax.experimental import pallas as pl
from jax.experimental.pallas import tpu as pltpu
from jax.sharding import PartitionSpec as P

HIGHEST = lax.Precision.HIGHEST
MESH = pl.DeviceIdType.MESH
TILE = 128


def transposed_product(left, right):
    return lax.dot_general(
        left,
        right,
        (((0,), (0,)), ((), ())),
        precision=HIGHEST,
        preferred_element_type=jnp.float32,
    )


def matrix_product(left, right):
    return jnp.dot(left, right, precision=HIGHEST, preferred_element_type=jnp.float32)


AXES = {"x": "x", "y": "y", "z": "z", "n": "near", "f": "far", "p": "plane"}
FIRST_ROUTES = ("xyz", "yxz", "zxy", "yxz", "xyz", "yxz", "yxz", "xyz")
FIRST_ORDER = (0, 1, 2, 3, 1, 0, 4, 5, 3, 2, 1, 0, 6, 7, 5, 4, 3, 2, 1, 0, 7, 6, 5, 4, 3, 2, 1, 0, 7, 6, 5, 4, 3, 2, 1, 0, 7, 6, 5, 4, 3, 2, 1, 0, 7, 6, 5, 4, 3, 2, 1, 0, -1, -2, 7, 6, 5, 4, 3, 2, -3, -4, -5, -6, 7, 6, -7, -8)
SECOND_ROUTES = ("pz", "zp")
SECOND_ORDER = (0, 1, 0, 1, 0, 1, 1, 0, 0, 1, 0, -1, 1, -2)


def plane_sides(chips):
    side = math.isqrt(chips)
    while chips % side:
        side -= 1
    return chips // side, side


class Piece:
    def __init__(self, tiles, order, chips):
        self.used = tiles
        self.tiles = -(-tiles // chips) * chips
        self.order = order
        self.step = 0


def make_plan(basis_columns, block_columns, sizes):
    chips = sizes["plane"] * sizes["z"]
    block = basis_columns // 4
    half = block_columns // 2
    square = block * block // 1024
    corner = half * half // 1024
    diagonal, corner = square - square // 4, corner - corner // 4
    shapes = [2 * diagonal, square, square, square] + [block * half // 1024] * 4
    first = [Piece(tiles, [AXES[letter] for letter in route], chips) for tiles, route in zip(shapes, FIRST_ROUTES)]
    second = [Piece(tiles, [AXES[letter] for letter in route], chips) for tiles, route in zip((corner, half * half // 2048), SECOND_ROUTES)]
    basis_gram, coeffs, gram = first[:4], first[4:], second
    place = dict(copy=0, source=0, held=0, partial=0)
    for group in (basis_gram, coeffs, gram):
        offset = 0
        for piece in group:
            piece.offset = offset
            offset += piece.tiles
            piece.source = place["source"]
            place["source"] += piece.tiles
            piece.stages = []
            size = piece.tiles
            for axis in piece.order:
                count = sizes[axis]
                size //= count
                stage = dict(axis=axis, size=size, held=place["held"], partial=place["partial"])
                stage["scatter"] = place["copy"]
                stage["gather"] = place["copy"] + count - 1
                place["copy"] += 2 * (count - 1)
                place["held"] += (count - 1) * size
                place["partial"] += size
                piece.stages.append(stage)
            piece.partner = place["copy"]
            place["copy"] += 1
    return basis_gram, coeffs, gram, place


def pieces_to_tiles(value):
    rows, cols = value.shape
    return [value[:, i : i + TILE].reshape(rows // 8, 8, TILE) for i in range(0, cols, TILE)]


def orthogonalize_kernel(
    plan,
    sizes,
    weight,
    counts_ref,
    basis_hbm,
    block_hbm,
    residual_ref,
    gram_ref,
    basis_ref,
    block_ref,
    load_sem,
    basis_all,
    block_half,
    block_send,
    source,
    held,
    partial,
    basis_gram_tiles,
    coeffs_tiles,
    gram_tiles,
    operator,
    correction,
    residual,
    send_sem,
    recv_sem,
    extra_send,
    extra_recv,
):
    basis_gram, coeffs, gram, _ = plan
    slots = basis_ref.shape[0]
    columns = basis_ref.shape[1]
    half = block_ref.shape[1] // 2
    block = columns // 4

    loads = [
        pltpu.make_async_copy(basis_hbm, basis_ref, load_sem.at[0]),
        pltpu.make_async_copy(block_hbm, block_ref, load_sem.at[1]),
    ]
    for copy in loads:
        copy.start()
    row = lax.axis_index("row")
    core = lax.rem(row, 2)
    chip = lax.div(row, 2)
    me = {
        "x": lax.rem(chip, sizes["x"]),
        "y": lax.div(chip, sizes["x"]),
        "z": lax.axis_index("grp"),
        "plane": chip,
        "near": lax.rem(lax.axis_index("grp"), sizes["near"]),
        "far": lax.div(lax.axis_index("grp"), sizes["near"]),
    }
    partner = {"row": row + 1 - 2 * core}

    def peer(axis, k):
        other = lax.rem(me[axis] + k, sizes[axis])
        if axis == "z":
            return {"grp": other}
        if axis == "near":
            return {"grp": me["far"] * sizes["near"] + other}
        if axis == "far":
            return {"grp": other * sizes["near"] + me["near"]}
        if axis == "plane":
            return {"row": other * 2 + core}
        x, y = (other, me["y"]) if axis == "x" else (me["x"], other)
        return {"row": (y * sizes["x"] + x) * 2 + core}

    barrier = pltpu.get_barrier_semaphore()
    pl.semaphore_signal(barrier, inc=1, device_id=partner, device_id_type=MESH)
    for axis in ("plane", "z"):
        for k in range(1, sizes[axis]):
            pl.semaphore_signal(barrier, inc=1, device_id=peer(axis, k), device_id_type=MESH)
    sent = []

    def start(source_ref, target_ref, sends, recvs, device):
        copy = pltpu.make_async_remote_copy(
            src_ref=source_ref,
            dst_ref=target_ref,
            send_sem=sends,
            recv_sem=recvs,
            device_id=device,
            device_id_type=MESH,
        )
        copy.start()
        sent.append(copy)
        return copy

    live = lax.broadcasted_iota(jnp.int32, (slots, 1), 0) < counts_ref[0, 0]
    mine = pl.ds(pl.multiple_of(core * slots, 8), slots)
    near = pl.ds(pl.multiple_of(core * half, TILE), half)
    far = pl.ds(pl.multiple_of((1 - core) * half, TILE), half)
    for copy in loads:
        copy.wait()
    basis_all[mine, :] = jnp.where(live, basis_ref[...], 0.0)
    block_send[...] = jnp.where(live, block_ref[:, far], 0.0)
    block_half[mine, :] = jnp.where(live, block_ref[:, near], 0.0)
    pl.semaphore_wait(barrier, sizes["plane"] + sizes["z"] - 1)
    shared = [
        start(basis_all.at[mine], basis_all.at[mine], extra_send.at[0], extra_recv.at[0], partner),
        start(block_send, block_half.at[mine], extra_send.at[1], extra_recv.at[1], partner),
    ]

    def position(piece, depth):
        offset = 0
        for stage in piece.stages[:depth]:
            offset = offset + me[stage["axis"]] * stage["size"]
        return offset

    def scatter(piece, depth):
        stage = piece.stages[depth]
        axis, size = stage["axis"], stage["size"]
        if depth == 0:
            base, ref = piece.source, source
        else:
            base, ref = piece.stages[depth - 1]["partial"], partial
        piece.waiting = []
        for k in range(1, sizes[axis]):
            chunk = lax.rem(me[axis] + k, sizes[axis]) * size
            index = stage["scatter"] + k - 1
            piece.waiting.append(
                start(
                    ref.at[pl.ds(base + chunk, size)],
                    held.at[pl.ds(stage["held"] + (k - 1) * size, size)],
                    send_sem.at[index],
                    recv_sem.at[index],
                    peer(axis, k),
                )
            )

    def reduced(piece, depth):
        stage = piece.stages[depth]
        axis, size = stage["axis"], stage["size"]
        if depth == 0:
            base, ref = piece.source, source
        else:
            base, ref = piece.stages[depth - 1]["partial"], partial
        for copy in piece.waiting:
            copy.wait_recv()
        total = ref[pl.ds(base + me[axis] * size, size)]
        for k in range(sizes[axis] - 1):
            total = total + held[pl.ds(stage["held"] + k * size, size)]
        return total

    def gather(piece, depth):
        stage = piece.stages[depth]
        axis = stage["axis"]
        place = piece.out.at[pl.ds(piece.offset + position(piece, depth + 1), stage["size"])]
        piece.waiting = []
        for k in range(1, sizes[axis]):
            index = stage["gather"] + k - 1
            piece.waiting.append(start(place, place, send_sem.at[index], recv_sem.at[index], peer(axis, k)))

    def stage_source(piece):
        offset = piece.source
        for value in piece.produce():
            source[pl.ds(offset, value.shape[0])] = value
            offset += value.shape[0]
        if piece.used < piece.tiles:
            source[pl.ds(offset, piece.tiles - piece.used)] = jnp.zeros(
                (piece.tiles - piece.used, 8, TILE), jnp.float32
            )

    def advance(piece):
        depth = len(piece.stages)
        step = piece.step
        piece.step += 1
        if step == 0:
            stage_source(piece)
            scatter(piece, 0)
            return
        if step < depth:
            stage = piece.stages[step - 1]
            partial[pl.ds(stage["partial"], stage["size"])] = reduced(piece, step - 1)
            scatter(piece, step)
            return
        if step == depth:
            size = piece.stages[-1]["size"]
            piece.out[pl.ds(piece.offset + position(piece, depth), size)] = reduced(piece, depth - 1)
            gather(piece, depth - 1)
            return
        for copy in piece.waiting:
            copy.wait_recv()
        piece.waiting = []
        if step < 2 * depth:
            gather(piece, 2 * depth - 1 - step)
        elif step == 2 * depth and piece.shared:
            place = piece.out.at[pl.ds(piece.offset, piece.tiles)]
            index = piece.partner
            piece.waiting = [start(place, place, send_sem.at[index], recv_sem.at[index], partner)]

    def run(pieces, order):
        for entry in order:
            if entry < 0:
                pieces[~entry].consume()
            else:
                advance(pieces[entry])

    def lanes(index, width):
        return pl.ds(pl.multiple_of(index * width, TILE), width)

    first, second = 2 * core, 2 * core + 1

    def basis_product(left, right):
        return transposed_product(basis_all[:, lanes(left, block)], basis_all[:, lanes(right, block)]) * weight

    def upper_tiles(value):
        middle = value.shape[0] // 2
        return pieces_to_tiles(value[:middle]) + pieces_to_tiles(value[middle:, middle:])

    def square_at(ref, offset, rows, cols):
        parts = [
            ref[pl.ds(offset + i * (rows // 8), rows // 8)].reshape(rows, TILE) for i in range(cols // TILE)
        ]
        return jnp.concatenate(parts, axis=1)

    def upper_at(ref, offset, size):
        middle = size // 2
        top = square_at(ref, offset, middle, size)
        corner = square_at(ref, offset + middle * size // 1024, middle, middle)
        return top, corner

    square = block * block // 1024

    def put_diagonal(owner, offset, index):
        top, corner = upper_at(basis_gram_tiles.at[owner], offset, block)
        middle = block // 2
        whole = jnp.concatenate([top, jnp.concatenate([top[:, middle:].T, corner], axis=1)], axis=0)
        unit = lax.broadcasted_iota(jnp.int32, whole.shape, 0) == lax.broadcasted_iota(jnp.int32, whole.shape, 1)
        window = slice(index * block, (index + 1) * block)
        operator[window, window] = jnp.where(unit, 1.0, 0.0) - whole

    def put_square(owner, offset, left, right):
        whole = -square_at(basis_gram_tiles.at[owner], offset, block, block)
        rows, cols = slice(left * block, (left + 1) * block), slice(right * block, (right + 1) * block)
        operator[rows, cols] = whole
        operator[cols, rows] = whole.T

    def consume_diagonals():
        offset = basis_gram[0].offset
        for owner in range(2):
            put_diagonal(owner, offset, 2 * owner)
            put_diagonal(owner, offset + square - square // 4, 2 * owner + 1)

    def consume_square(piece, pairs):
        for owner, (left, right) in enumerate(pairs):
            put_square(owner, piece.offset, left, right)

    def produce_coeffs(index):
        return pieces_to_tiles(
            transposed_product(basis_all[:, index * block : (index + 1) * block], block_half[...]) * weight
        )

    def consume_coeffs(index):
        piece = coeffs[index]
        value = square_at(coeffs_tiles, piece.offset, block, half)
        window = slice(index * block, (index + 1) * block)
        change = matrix_product(operator[:, window], value)
        removed = matrix_product(basis_all[:, window], value)
        if index == 0:
            correction[...] = change
            residual[core] = block_half[...] - removed
        else:
            correction[...] += change
            residual[core] -= removed

    for piece in basis_gram:
        piece.out, piece.shared = basis_gram_tiles.at[core], True
    for piece in coeffs:
        piece.out, piece.shared = coeffs_tiles, False
    for piece in gram:
        piece.out, piece.shared = gram_tiles.at[core], True
    basis_gram[0].produce = lambda: upper_tiles(basis_product(first, first)) + upper_tiles(
        basis_product(second, second)
    )
    basis_gram[1].produce = lambda: pieces_to_tiles(basis_product(first, second))
    basis_gram[2].produce = lambda: pieces_to_tiles(basis_product(second, lax.rem(second + 1, 4)))
    basis_gram[3].produce = lambda: pieces_to_tiles(basis_product(core, core + 2))
    basis_gram[0].consume = consume_diagonals
    basis_gram[1].consume = lambda: consume_square(basis_gram[1], ((0, 1), (2, 3)))
    basis_gram[2].consume = lambda: consume_square(basis_gram[2], ((1, 2), (3, 0)))
    basis_gram[3].consume = lambda: consume_square(basis_gram[3], ((0, 2), (1, 3)))
    for index, piece in enumerate(coeffs):
        piece.produce = functools.partial(produce_coeffs, index)
        piece.consume = functools.partial(consume_coeffs, index)

    for copy in shared:
        copy.wait_recv()
    run(basis_gram + coeffs, FIRST_ORDER)

    residual[core] -= matrix_product(basis_all[...], correction[...])
    swap = start(residual.at[core], residual.at[core], extra_send.at[2], extra_recv.at[2], partner)

    gram_ref[...] = jnp.zeros_like(gram_ref)

    def produce_cross():
        swap.wait_recv()
        left = residual[0, :, lanes(core, half // 2)]
        return pieces_to_tiles(transposed_product(left, residual[1]) * weight)

    def consume_corners():
        for owner in range(2):
            top, corner = upper_at(gram_tiles.at[owner], gram[0].offset, half)
            middle, base = half // 2, owner * half
            gram_ref[base : base + middle, base : base + half] = top
            gram_ref[base + middle : base + half, base + middle : base + half] = corner

    def consume_cross():
        middle = half // 2
        for owner in range(2):
            gram_ref[owner * middle : (owner + 1) * middle, half:] = square_at(
                gram_tiles.at[owner], gram[1].offset, middle, half
            )

    gram[0].produce = lambda: upper_tiles(transposed_product(residual[core], residual[core]) * weight)
    gram[0].consume = consume_corners
    gram[1].produce = produce_cross
    gram[1].consume = consume_cross
    run(gram, SECOND_ORDER)
    for owner in range(2):
        residual_ref[:, owner * half : (owner + 1) * half] = residual[owner, mine, :]
    for copy in sent:
        copy.wait_send()


def orthogonalize(basis, block, counts):
    slots, columns = basis.shape
    width = block.shape[1]
    row_size, grp_size = lax.axis_size("row"), lax.axis_size("grp")
    across, down = plane_sides(row_size // 2)
    near = 2 - grp_size % 2
    sizes = {"x": across, "y": down, "z": grp_size, "plane": across * down, "near": near, "far": grp_size // near}
    plan = make_plan(columns, width, sizes)
    basis_gram, coeffs, gram, place = plan
    weight = 1.0 / (slots * row_size * grp_size)
    half = width // 2
    vmem = pl.BlockSpec(memory_space=pltpu.VMEM)

    def tiles(*shape):
        return pltpu.VMEM(shape + (8, TILE), jnp.float32)

    def total(group):
        return sum(piece.tiles for piece in group)

    return pl.pallas_call(
        functools.partial(orthogonalize_kernel, plan, sizes, weight),
        out_shape=(
            jax.ShapeDtypeStruct((slots, width), jnp.float32),
            jax.ShapeDtypeStruct((width, width), jnp.float32),
        ),
        in_specs=[pl.BlockSpec(memory_space=pltpu.SMEM)] + [pl.BlockSpec(memory_space=pl.ANY)] * 2,
        out_specs=(vmem, vmem),
        scratch_shapes=[
            pltpu.VMEM((slots, columns), jnp.float32),
            pltpu.VMEM((slots, width), jnp.float32),
            pltpu.SemaphoreType.DMA((2,)),
            pltpu.VMEM((2 * slots, columns), jnp.float32),
            pltpu.VMEM((2 * slots, half), jnp.float32),
            pltpu.VMEM((slots, half), jnp.float32),
            tiles(place["source"]),
            tiles(place["held"]),
            tiles(place["partial"]),
            tiles(2, total(basis_gram)),
            tiles(total(coeffs)),
            tiles(2, total(gram)),
            pltpu.VMEM((columns, columns), jnp.float32),
            pltpu.VMEM((columns, half), jnp.float32),
            pltpu.VMEM((2, 2 * slots, half), jnp.float32),
            pltpu.SemaphoreType.DMA((place["copy"],)),
            pltpu.SemaphoreType.DMA((place["copy"],)),
            pltpu.SemaphoreType.DMA((3,)),
            pltpu.SemaphoreType.DMA((3,)),
        ],
        compiler_params=pltpu.CompilerParams(collective_id=0, has_side_effects=True),
        name="orthogonalize",
    )(counts, basis, block)


BLOCK = 64
GROUP = 8


BLOCK = 64
GROUP = 8


def eliminate(square):
    size = square.shape[0]
    count = size // GROUP
    shape = (GROUP, 2 * size)
    sub = lax.broadcasted_iota(jnp.int32, shape, 0)
    lane = lax.broadcasted_iota(jnp.int32, shape, 1)
    wide = [
        jnp.concatenate(
            [
                square[GROUP * b : GROUP * (b + 1)],
                (lane[:, :size] == sub[:, :size] + GROUP * b).astype(jnp.float32),
            ],
            axis=1,
        )
        for b in range(count)
    ]

    def across(value, index):
        return jnp.broadcast_to(value[:, index : index + 1], shape)

    def down(value, index):
        return jnp.broadcast_to(value[index : index + 1], shape)

    roots = []
    for g in range(count):
        columns = {b: [across(wide[b], GROUP * g + i) for i in range(GROUP)] for b in range(g, count)}
        columns[g] = [jnp.where(lane < 2 * size, column, 0.0) for column in columns[g]]
        pivots = jnp.ones(shape, jnp.float32)
        for i in range(GROUP):
            pivot = down(columns[g][i], i)
            inverse = 1.0 / pivot
            pivots = jnp.where(sub == i, pivot, pivots)
            later = [down(columns[g][j], i) for j in range(i + 1, GROUP)]
            row = down(wide[g], i)
            for b in range(g, count):
                if b == g and i == GROUP - 1:
                    continue
                column = jnp.where(sub > i, columns[b][i], 0.0) if b == g else columns[b][i]
                factor = column * inverse
                for j in range(i + 1, GROUP):
                    columns[b][j] = columns[b][j] - factor * later[j - i - 1]
                wide[b] = wide[b] - factor * row
        roots.append(lax.rsqrt(pivots))
    upper, inverted = [], []
    for b in range(count):
        value = wide[b] * roots[b]
        upper.append(jnp.where((lane >= sub + GROUP * b)[:, :size], value[:, :size], 0.0))
        inverted.append(jnp.where((lane <= sub + GROUP * b)[:, :size], value[:, size:], 0.0))
    return jnp.concatenate(upper, axis=0), jnp.concatenate(inverted, axis=0)


def factor_kernel(gram_ref, residual_ref, new_ref, factor_ref, work, rest):
    size = gram_ref.shape[0]
    steps = size // BLOCK
    work[...] = gram_ref[...]
    rest[...] = residual_ref[...]
    square = work[:BLOCK, :BLOCK]
    for step in range(steps):
        here, after, beyond = (BLOCK * (step + i) for i in range(3))
        upper, inverted = eliminate(square)
        if step:
            factor_ref[here:after, :here] = jnp.zeros((BLOCK, here), jnp.float32)
        factor_ref[here:after, here:after] = upper
        if after < size:
            near = matrix_product(inverted, work[here:after, after:beyond])
            square = work[after:beyond, after:beyond] - transposed_product(near, near)
            factor_ref[here:after, after:beyond] = near
            if beyond < size:
                panel = matrix_product(inverted, work[here:after, beyond:])
                factor_ref[here:after, beyond:] = panel
                work[after:beyond, beyond:] -= transposed_product(near, panel)
                for start in range(beyond, size, 2 * BLOCK):
                    stop = min(start + 2 * BLOCK, size)
                    work[start:stop, start:] -= transposed_product(
                        panel[:, start - beyond : stop - beyond], panel[:, start - beyond :]
                    )
        solved = lax.dot_general(
            rest[:, here:after],
            inverted,
            (((1,), (1,)), ((), ())),
            precision=HIGHEST,
            preferred_element_type=jnp.float32,
        )
        new_ref[:, here:after] = solved
        if after < size:
            rest[:, after:] -= matrix_product(solved, factor_ref[here:after, after:])


def factor_and_solve(gram, residual):
    vmem = pl.BlockSpec(memory_space=pltpu.VMEM)
    return pl.pallas_call(
        factor_kernel,
        out_shape=(
            jax.ShapeDtypeStruct(residual.shape, jnp.float32),
            jax.ShapeDtypeStruct(gram.shape, jnp.float32),
        ),
        in_specs=[vmem, vmem],
        out_specs=(vmem, vmem),
        scratch_shapes=[pltpu.VMEM(gram.shape, jnp.float32), pltpu.VMEM(residual.shape, jnp.float32)],
        name="factor_and_solve",
    )(gram, residual)


def body(basis, block, counts):
    residual, gram = orthogonalize(basis, block, counts)
    return factor_and_solve(gram, residual)


def solution(mesh):
    placed = (P(("grp", "row"), None), P(("grp", "row"), None), P("grp", "row"))
    return jax.shard_map(
        body, mesh=mesh, in_specs=placed, out_specs=(P(("grp", "row"), None), P()), check_vma=False
    )
```

```python
import functools
import math

import jax
import jax.numpy as jnp
from jax import lax
from jax.experimental import pallas as pl
from jax.experimental.pallas import tpu as pltpu
from jax.sharding import PartitionSpec as P

HIGHEST = lax.Precision.HIGHEST
MESH = pl.DeviceIdType.MESH
TILE = 128


def transposed_product(left, right):
    return lax.dot_general(
        left,
        right,
        (((0,), (0,)), ((), ())),
        precision=HIGHEST,
        preferred_element_type=jnp.float32,
    )


def matrix_product(left, right):
    return jnp.dot(left, right, precision=HIGHEST, preferred_element_type=jnp.float32)


AXES = {"x": "x", "y": "y", "z": "z", "n": "near", "f": "far", "p": "plane"}
FIRST_ROUTES = ("xyz", "yxz", "zxy", "yxz", "xyz", "yxz", "yxz", "xyz")
FIRST_ORDER = (0, 1, 2, 3, 1, 0, 4, 5, 3, 2, 1, 0, 6, 7, 5, 4, 3, 2, 1, 0, 7, 6, 5, 4, 3, 2, 1, 0, 7, 6, 5, 4, 3, 2, 1, 0, 7, 6, 5, 4, 3, 2, 1, 0, 7, 6, 5, 4, 3, 2, 1, 0, -1, -2, 7, 6, 5, 4, 3, 2, -3, -4, -5, -6, 7, 6, -7, -8)
SECOND_ROUTES = ("pz", "zp")
SECOND_ORDER = (0, 1, 0, 1, 0, 1, 1, 0, 0, 1, 0, -1, 1, -2)


def plane_sides(chips):
    side = math.isqrt(chips)
    while chips % side:
        side -= 1
    return chips // side, side


class Piece:
    def __init__(self, tiles, order, chips):
        self.used = tiles
        self.tiles = -(-tiles // chips) * chips
        self.order = order
        self.step = 0


def make_plan(basis_columns, block_columns, sizes):
    chips = sizes["plane"] * sizes["z"]
    block = basis_columns // 4
    half = block_columns // 2
    square = block * block // 1024
    corner = half * half // 1024
    diagonal, corner = square - square // 4, corner - corner // 4
    shapes = [2 * diagonal, square, square, square] + [block * half // 1024] * 4
    first = [Piece(tiles, [AXES[letter] for letter in route], chips) for tiles, route in zip(shapes, FIRST_ROUTES)]
    second = [Piece(tiles, [AXES[letter] for letter in route], chips) for tiles, route in zip((corner, half * half // 2048), SECOND_ROUTES)]
    basis_gram, coeffs, gram = first[:4], first[4:], second
    place = dict(copy=0, source=0, held=0, partial=0)
    for group in (basis_gram, coeffs, gram):
        offset = 0
        for piece in group:
            piece.offset = offset
            offset += piece.tiles
            piece.source = place["source"]
            place["source"] += piece.tiles
            piece.stages = []
            size = piece.tiles
            for axis in piece.order:
                count = sizes[axis]
                size //= count
                stage = dict(axis=axis, size=size, held=place["held"], partial=place["partial"])
                stage["scatter"] = place["copy"]
                stage["gather"] = place["copy"] + count - 1
                place["copy"] += 2 * (count - 1)
                place["held"] += (count - 1) * size
                place["partial"] += size
                piece.stages.append(stage)
            piece.partner = place["copy"]
            place["copy"] += 1
    return basis_gram, coeffs, gram, place


def pieces_to_tiles(value):
    rows, cols = value.shape
    return [value[:, i : i + TILE].reshape(rows // 8, 8, TILE) for i in range(0, cols, TILE)]


def orthogonalize_kernel(
    plan,
    sizes,
    weight,
    counts_ref,
    basis_hbm,
    block_hbm,
    residual_hbm,
    gram_ref,
    basis_ref,
    block_ref,
    load_sem,
    store_sem,
    basis_all,
    block_half,
    block_send,
    source,
    held,
    partial,
    basis_gram_tiles,
    coeffs_tiles,
    gram_tiles,
    operator,
    correction,
    residual,
    send_sem,
    recv_sem,
    extra_send,
    extra_recv,
):
    basis_gram, coeffs, gram, _ = plan
    slots = basis_ref.shape[0]
    columns = basis_ref.shape[1]
    half = block_ref.shape[1] // 2
    block = columns // 4

    loads = [
        pltpu.make_async_copy(basis_hbm, basis_ref, load_sem.at[0]),
        pltpu.make_async_copy(block_hbm, block_ref, load_sem.at[1]),
    ]
    for copy in loads:
        copy.start()
    row = lax.axis_index("row")
    core = lax.rem(row, 2)
    chip = lax.div(row, 2)
    me = {
        "x": lax.rem(chip, sizes["x"]),
        "y": lax.div(chip, sizes["x"]),
        "z": lax.axis_index("grp"),
        "plane": chip,
        "near": lax.rem(lax.axis_index("grp"), sizes["near"]),
        "far": lax.div(lax.axis_index("grp"), sizes["near"]),
    }
    partner = {"row": row + 1 - 2 * core}

    def peer(axis, k):
        other = lax.rem(me[axis] + k, sizes[axis])
        if axis == "z":
            return {"grp": other}
        if axis == "near":
            return {"grp": me["far"] * sizes["near"] + other}
        if axis == "far":
            return {"grp": other * sizes["near"] + me["near"]}
        if axis == "plane":
            return {"row": other * 2 + core}
        x, y = (other, me["y"]) if axis == "x" else (me["x"], other)
        return {"row": (y * sizes["x"] + x) * 2 + core}

    barrier = pltpu.get_barrier_semaphore()
    pl.semaphore_signal(barrier, inc=1, device_id=partner, device_id_type=MESH)
    for axis in ("plane", "z"):
        for k in range(1, sizes[axis]):
            pl.semaphore_signal(barrier, inc=1, device_id=peer(axis, k), device_id_type=MESH)
    sent = []

    def start(source_ref, target_ref, sends, recvs, device):
        copy = pltpu.make_async_remote_copy(
            src_ref=source_ref,
            dst_ref=target_ref,
            send_sem=sends,
            recv_sem=recvs,
            device_id=device,
            device_id_type=MESH,
        )
        copy.start()
        sent.append(copy)
        return copy

    live = lax.broadcasted_iota(jnp.int32, (slots, 1), 0) < counts_ref[0, 0]
    mine = pl.ds(pl.multiple_of(core * slots, 8), slots)
    near = pl.ds(pl.multiple_of(core * half, TILE), half)
    far = pl.ds(pl.multiple_of((1 - core) * half, TILE), half)
    for copy in loads:
        copy.wait()
    basis_all[mine, :] = jnp.where(live, basis_ref[...], 0.0)
    block_send[...] = jnp.where(live, block_ref[:, far], 0.0)
    block_half[mine, :] = jnp.where(live, block_ref[:, near], 0.0)
    pl.semaphore_wait(barrier, sizes["plane"] + sizes["z"] - 1)
    wide = columns // 2
    shared = []
    for index, side in enumerate((1 - core, core)):
        place = basis_all.at[mine, pl.ds(pl.multiple_of(side * wide, TILE), wide)]
        shared.append(start(place, place, extra_send.at[index], extra_recv.at[index], partner))
    shared.append(start(block_send, block_half.at[mine], extra_send.at[3], extra_recv.at[3], partner))

    def position(piece, depth):
        offset = 0
        for stage in piece.stages[:depth]:
            offset = offset + me[stage["axis"]] * stage["size"]
        return offset

    def scatter(piece, depth):
        stage = piece.stages[depth]
        axis, size = stage["axis"], stage["size"]
        if depth == 0:
            base, ref = piece.source, source
        else:
            base, ref = piece.stages[depth - 1]["partial"], partial
        piece.waiting = []
        for k in range(1, sizes[axis]):
            chunk = lax.rem(me[axis] + k, sizes[axis]) * size
            index = stage["scatter"] + k - 1
            piece.waiting.append(
                start(
                    ref.at[pl.ds(base + chunk, size)],
                    held.at[pl.ds(stage["held"] + (k - 1) * size, size)],
                    send_sem.at[index],
                    recv_sem.at[index],
                    peer(axis, k),
                )
            )

    def reduced(piece, depth):
        stage = piece.stages[depth]
        axis, size = stage["axis"], stage["size"]
        if depth == 0:
            base, ref = piece.source, source
        else:
            base, ref = piece.stages[depth - 1]["partial"], partial
        for copy in piece.waiting:
            copy.wait_recv()
        total = ref[pl.ds(base + me[axis] * size, size)]
        for k in range(sizes[axis] - 1):
            total = total + held[pl.ds(stage["held"] + k * size, size)]
        return total

    def gather(piece, depth):
        stage = piece.stages[depth]
        axis = stage["axis"]
        place = piece.out.at[pl.ds(piece.offset + position(piece, depth + 1), stage["size"])]
        piece.waiting = []
        for k in range(1, sizes[axis]):
            index = stage["gather"] + k - 1
            piece.waiting.append(start(place, place, send_sem.at[index], recv_sem.at[index], peer(axis, k)))

    def stage_source(piece):
        offset = piece.source
        for value in piece.produce():
            source[pl.ds(offset, value.shape[0])] = value
            offset += value.shape[0]
        if piece.used < piece.tiles:
            source[pl.ds(offset, piece.tiles - piece.used)] = jnp.zeros(
                (piece.tiles - piece.used, 8, TILE), jnp.float32
            )

    def advance(piece):
        depth = len(piece.stages)
        step = piece.step
        piece.step += 1
        if step == 0:
            stage_source(piece)
            scatter(piece, 0)
            return
        if step < depth:
            stage = piece.stages[step - 1]
            partial[pl.ds(stage["partial"], stage["size"])] = reduced(piece, step - 1)
            scatter(piece, step)
            return
        if step == depth:
            size = piece.stages[-1]["size"]
            piece.out[pl.ds(piece.offset + position(piece, depth), size)] = reduced(piece, depth - 1)
            gather(piece, depth - 1)
            return
        for copy in piece.waiting:
            copy.wait_recv()
        piece.waiting = []
        if step < 2 * depth:
            gather(piece, 2 * depth - 1 - step)
        elif step == 2 * depth and piece.shared:
            place = piece.out.at[pl.ds(piece.offset, piece.tiles)]
            index = piece.partner
            piece.waiting = [start(place, place, send_sem.at[index], recv_sem.at[index], partner)]

    def run(pieces, order):
        for entry in order:
            if entry < 0:
                pieces[~entry].consume()
            else:
                advance(pieces[entry])

    def lanes(index, width):
        return pl.ds(pl.multiple_of(index * width, TILE), width)

    first, second = 2 * core, 2 * core + 1

    def basis_product(left, right):
        return transposed_product(basis_all[:, lanes(left, block)], basis_all[:, lanes(right, block)]) * weight

    def upper_tiles(value):
        middle = value.shape[0] // 2
        return pieces_to_tiles(value[:middle]) + pieces_to_tiles(value[middle:, middle:])

    def square_at(ref, offset, rows, cols):
        parts = [
            ref[pl.ds(offset + i * (rows // 8), rows // 8)].reshape(rows, TILE) for i in range(cols // TILE)
        ]
        return jnp.concatenate(parts, axis=1)

    def upper_at(ref, offset, size):
        middle = size // 2
        top = square_at(ref, offset, middle, size)
        corner = square_at(ref, offset + middle * size // 1024, middle, middle)
        return top, corner

    square = block * block // 1024

    def put_diagonal(owner, offset, index):
        top, corner = upper_at(basis_gram_tiles.at[owner], offset, block)
        middle = block // 2
        whole = jnp.concatenate([top, jnp.concatenate([top[:, middle:].T, corner], axis=1)], axis=0)
        unit = lax.broadcasted_iota(jnp.int32, whole.shape, 0) == lax.broadcasted_iota(jnp.int32, whole.shape, 1)
        window = slice(index * block, (index + 1) * block)
        operator[window, window] = jnp.where(unit, 1.0, 0.0) - whole

    def put_square(owner, offset, left, right):
        whole = -square_at(basis_gram_tiles.at[owner], offset, block, block)
        rows, cols = slice(left * block, (left + 1) * block), slice(right * block, (right + 1) * block)
        operator[rows, cols] = whole
        operator[cols, rows] = whole.T

    def consume_diagonals():
        offset = basis_gram[0].offset
        for owner in range(2):
            put_diagonal(owner, offset, 2 * owner)
            put_diagonal(owner, offset + square - square // 4, 2 * owner + 1)

    def consume_square(piece, pairs):
        for owner, (left, right) in enumerate(pairs):
            put_square(owner, piece.offset, left, right)

    def produce_coeffs(index):
        return pieces_to_tiles(
            transposed_product(basis_all[:, index * block : (index + 1) * block], block_half[...]) * weight
        )

    def consume_coeffs(index):
        piece = coeffs[index]
        value = square_at(coeffs_tiles, piece.offset, block, half)
        window = slice(index * block, (index + 1) * block)
        change = matrix_product(operator[:, window], value)
        removed = matrix_product(basis_all[:, window], value)
        if index == 0:
            correction[...] = change
            residual[core] = block_half[...] - removed
        else:
            correction[...] += change
            residual[core] -= removed

    for piece in basis_gram:
        piece.out, piece.shared = basis_gram_tiles.at[core], True
    for piece in coeffs:
        piece.out, piece.shared = coeffs_tiles, False
    for piece in gram:
        piece.out, piece.shared = gram_tiles.at[core], True
    def produce_diagonals():
        shared[0].wait_recv()
        return upper_tiles(basis_product(first, first)) + upper_tiles(basis_product(second, second))

    def produce_beyond():
        shared[1].wait_recv()
        shared[2].wait_recv()
        return pieces_to_tiles(basis_product(second, lax.rem(second + 1, 4)))

    basis_gram[0].produce = produce_diagonals
    basis_gram[1].produce = lambda: pieces_to_tiles(basis_product(first, second))
    basis_gram[2].produce = produce_beyond
    basis_gram[3].produce = lambda: pieces_to_tiles(basis_product(core, core + 2))
    basis_gram[0].consume = consume_diagonals
    basis_gram[1].consume = lambda: consume_square(basis_gram[1], ((0, 1), (2, 3)))
    basis_gram[2].consume = lambda: consume_square(basis_gram[2], ((1, 2), (3, 0)))
    basis_gram[3].consume = lambda: consume_square(basis_gram[3], ((0, 2), (1, 3)))
    for index, piece in enumerate(coeffs):
        piece.produce = functools.partial(produce_coeffs, index)
        piece.consume = functools.partial(consume_coeffs, index)

    run(basis_gram + coeffs, FIRST_ORDER)

    residual[core] -= matrix_product(basis_all[...], correction[...])
    stores = [
        pltpu.make_async_copy(
            residual.at[owner, mine],
            residual_hbm.at[:, owner * half : (owner + 1) * half],
            store_sem.at[owner],
        )
        for owner in range(2)
    ]
    swap = start(residual.at[core], residual.at[core], extra_send.at[2], extra_recv.at[2], partner)

    gram_ref[...] = jnp.zeros_like(gram_ref)

    def produce_cross():
        swap.wait_recv()
        for copy in stores:
            copy.start()
        left = residual[0, :, lanes(core, half // 2)]
        return pieces_to_tiles(transposed_product(left, residual[1]) * weight)

    def consume_corners():
        for owner in range(2):
            top, corner = upper_at(gram_tiles.at[owner], gram[0].offset, half)
            middle, base = half // 2, owner * half
            gram_ref[base : base + middle, base : base + half] = top
            gram_ref[base + middle : base + half, base + middle : base + half] = corner

    def consume_cross():
        middle = half // 2
        for owner in range(2):
            gram_ref[owner * middle : (owner + 1) * middle, half:] = square_at(
                gram_tiles.at[owner], gram[1].offset, middle, half
            )

    gram[0].produce = lambda: upper_tiles(transposed_product(residual[core], residual[core]) * weight)
    gram[0].consume = consume_corners
    gram[1].produce = produce_cross
    gram[1].consume = consume_cross
    run(gram, SECOND_ORDER)
    for copy in stores:
        copy.wait()
    for copy in sent:
        copy.wait_send()


def orthogonalize(basis, block, counts):
    slots, columns = basis.shape
    width = block.shape[1]
    row_size, grp_size = lax.axis_size("row"), lax.axis_size("grp")
    across, down = plane_sides(row_size // 2)
    near = 2 - grp_size % 2
    sizes = {"x": across, "y": down, "z": grp_size, "plane": across * down, "near": near, "far": grp_size // near}
    plan = make_plan(columns, width, sizes)
    basis_gram, coeffs, gram, place = plan
    weight = 1.0 / (slots * row_size * grp_size)
    half = width // 2
    vmem = pl.BlockSpec(memory_space=pltpu.VMEM)

    def tiles(*shape):
        return pltpu.VMEM(shape + (8, TILE), jnp.float32)

    def total(group):
        return sum(piece.tiles for piece in group)

    return pl.pallas_call(
        functools.partial(orthogonalize_kernel, plan, sizes, weight),
        out_shape=(
            jax.ShapeDtypeStruct((slots, width), jnp.float32),
            jax.ShapeDtypeStruct((width, width), jnp.float32),
        ),
        in_specs=[pl.BlockSpec(memory_space=pltpu.SMEM)] + [pl.BlockSpec(memory_space=pl.ANY)] * 2,
        out_specs=(pl.BlockSpec(memory_space=pl.ANY), vmem),
        scratch_shapes=[
            pltpu.VMEM((slots, columns), jnp.float32),
            pltpu.VMEM((slots, width), jnp.float32),
            pltpu.SemaphoreType.DMA((2,)),
            pltpu.SemaphoreType.DMA((2,)),
            pltpu.VMEM((2 * slots, columns), jnp.float32),
            pltpu.VMEM((2 * slots, half), jnp.float32),
            pltpu.VMEM((slots, half), jnp.float32),
            tiles(place["source"]),
            tiles(place["held"]),
            tiles(place["partial"]),
            tiles(2, total(basis_gram)),
            tiles(total(coeffs)),
            tiles(2, total(gram)),
            pltpu.VMEM((columns, columns), jnp.float32),
            pltpu.VMEM((columns, half), jnp.float32),
            pltpu.VMEM((2, 2 * slots, half), jnp.float32),
            pltpu.SemaphoreType.DMA((place["copy"],)),
            pltpu.SemaphoreType.DMA((place["copy"],)),
            pltpu.SemaphoreType.DMA((4,)),
            pltpu.SemaphoreType.DMA((4,)),
        ],
        compiler_params=pltpu.CompilerParams(collective_id=0, has_side_effects=True),
        name="orthogonalize",
    )(counts, basis, block)


BLOCK = 64
GROUP = 8


def eliminate(square):
    size = square.shape[0]
    count = size // GROUP
    shape = (GROUP, 2 * size)
    sub = lax.broadcasted_iota(jnp.int32, shape, 0)
    lane = lax.broadcasted_iota(jnp.int32, shape, 1)
    wide = [
        jnp.concatenate(
            [
                square[GROUP * b : GROUP * (b + 1)],
                (lane[:, :size] == sub[:, :size] + GROUP * b).astype(jnp.float32),
            ],
            axis=1,
        )
        for b in range(count)
    ]

    def across(value, index):
        return jnp.broadcast_to(value[:, index : index + 1], shape)

    def down(value, index):
        return jnp.broadcast_to(value[index : index + 1], shape)

    roots = []

    def shown(value):
        return jnp.where(lane < 2 * size, value, 0.0)

    home = [shown(across(wide[0], i)) for i in range(GROUP)]
    for g in range(count):
        columns = {b: [across(wide[b], GROUP * g + i) for i in range(GROUP)] for b in range(g + 1, count)}
        columns[g] = home
        if g + 1 < count:
            ahead = {b: [shown(across(wide[b], GROUP * (g + 1) + i)) for i in range(GROUP)] for b in (g, g + 1)}
        pivots = jnp.ones(shape, jnp.float32)
        for i in range(GROUP):
            pivot = down(columns[g][i], i)
            inverse = 1.0 / pivot
            pivots = jnp.where(sub == i, pivot, pivots)
            later = [down(columns[g][j], i) for j in range(i + 1, GROUP)]
            row = down(wide[g], i)
            if g + 1 < count:
                cross = [down(value, i) for value in ahead[g]]
            for b in range(g, count):
                if b == g and i == GROUP - 1:
                    continue
                column = jnp.where(sub > i, columns[b][i], 0.0) if b == g else columns[b][i]
                factor = column * inverse
                for j in range(i + 1, GROUP):
                    columns[b][j] = columns[b][j] - factor * later[j - i - 1]
                wide[b] = wide[b] - factor * row
                if g + 1 < count and b <= g + 1:
                    ahead[b] = [value - factor * over for value, over in zip(ahead[b], cross)]
        if g + 1 < count:
            home = ahead[g + 1]
        roots.append(lax.rsqrt(pivots))
    upper, inverted = [], []
    for b in range(count):
        value = wide[b] * roots[b]
        upper.append(jnp.where((lane >= sub + GROUP * b)[:, :size], value[:, :size], 0.0))
        inverted.append(jnp.where((lane <= sub + GROUP * b)[:, :size], value[:, size:], 0.0))
    return jnp.concatenate(upper, axis=0), jnp.concatenate(inverted, axis=0)


def factor_kernel(gram_hbm, residual_hbm, new_hbm, factor_hbm, work, rest, new_ref, factor_ref, load_sem, store_sem):
    size = gram_hbm.shape[0]
    steps = size // BLOCK
    loads = [
        pltpu.make_async_copy(gram_hbm.at[:BLOCK], work.at[:BLOCK], load_sem.at[0]),
        pltpu.make_async_copy(gram_hbm.at[BLOCK:], work.at[BLOCK:], load_sem.at[1]),
        pltpu.make_async_copy(residual_hbm, rest, load_sem.at[2]),
    ]
    for copy in loads:
        copy.start()
    stores = []

    def store(source, target):
        copy = pltpu.make_async_copy(source, target, store_sem.at[len(stores)])
        copy.start()
        stores.append(copy)

    loads[0].wait()
    square = work[:BLOCK, :BLOCK]
    for step in range(steps):
        here, after, beyond = (BLOCK * (step + i) for i in range(3))
        upper, inverted = eliminate(square)
        if step == 0:
            loads[1].wait()
            loads[2].wait()
        if step:
            factor_ref[here:after, :here] = jnp.zeros((BLOCK, here), jnp.float32)
        factor_ref[here:after, here:after] = upper
        if after < size:
            near = matrix_product(inverted, work[here:after, after:beyond])
            square = work[after:beyond, after:beyond] - transposed_product(near, near)
            factor_ref[here:after, after:beyond] = near
            if beyond < size:
                panel = matrix_product(inverted, work[here:after, beyond:])
                factor_ref[here:after, beyond:] = panel
                work[after:beyond, beyond:] -= transposed_product(near, panel)
                for start in range(beyond, size, 2 * BLOCK):
                    stop = min(start + 2 * BLOCK, size)
                    work[start:stop, start:] -= transposed_product(
                        panel[:, start - beyond : stop - beyond], panel[:, start - beyond :]
                    )
        solved = lax.dot_general(
            rest[:, here:after],
            inverted,
            (((1,), (1,)), ((), ())),
            precision=HIGHEST,
            preferred_element_type=jnp.float32,
        )
        new_ref[:, here:after] = solved
        store(factor_ref.at[here:after], factor_hbm.at[here:after])
        if after % TILE == 0:
            store(new_ref.at[:, after - TILE : after], new_hbm.at[:, after - TILE : after])
        if after < size:
            rest[:, after:] -= matrix_product(solved, factor_ref[here:after, after:])
    for copy in stores:
        copy.wait()


def factor_and_solve(gram, residual):
    hbm = pl.BlockSpec(memory_space=pl.ANY)
    copies = gram.shape[0] // BLOCK + gram.shape[0] // TILE
    return pl.pallas_call(
        factor_kernel,
        out_shape=(
            jax.ShapeDtypeStruct(residual.shape, jnp.float32),
            jax.ShapeDtypeStruct(gram.shape, jnp.float32),
        ),
        in_specs=[hbm, hbm],
        out_specs=(hbm, hbm),
        scratch_shapes=[
            pltpu.VMEM(gram.shape, jnp.float32),
            pltpu.VMEM(residual.shape, jnp.float32),
            pltpu.VMEM(residual.shape, jnp.float32),
            pltpu.VMEM(gram.shape, jnp.float32),
            pltpu.SemaphoreType.DMA((3,)),
            pltpu.SemaphoreType.DMA((copies,)),
        ],
        name="factor_and_solve",
    )(gram, residual)


def body(basis, block, counts):
    residual, gram = orthogonalize(basis, block, counts)
    return factor_and_solve(gram, residual)


def solution(mesh):
    placed = (P(("grp", "row"), None), P(("grp", "row"), None), P("grp", "row"))
    return jax.shard_map(
        body, mesh=mesh, in_specs=placed, out_specs=(P(("grp", "row"), None), P()), check_vma=False
    )
```

```python
import functools
import math

import jax
import jax.numpy as jnp
from jax import lax
from jax.experimental import pallas as pl
from jax.experimental.pallas import tpu as pltpu
from jax.sharding import PartitionSpec as P

HIGHEST = lax.Precision.HIGHEST
MESH = pl.DeviceIdType.MESH
TILE = 128


def transposed_product(left, right):
    return lax.dot_general(
        left,
        right,
        (((0,), (0,)), ((), ())),
        precision=HIGHEST,
        preferred_element_type=jnp.float32,
    )


def matrix_product(left, right):
    return jnp.dot(left, right, precision=HIGHEST, preferred_element_type=jnp.float32)


AXES = {"x": "x", "y": "y", "z": "z", "n": "near", "f": "far", "p": "plane"}
FIRST_ROUTES = ("xyz", "yxz", "zxy", "yxz", "xyz", "yxz", "yxz", "xyz")
FIRST_ORDER = (0, 1, 2, 3, 1, 0, 4, 5, 3, 2, 1, 0, 6, 7, 5, 4, 3, 2, 1, 0, 7, 6, 5, 4, 3, 2, 1, 0, 7, 6, 5, 4, 3, 2, 1, 0, 7, 6, 5, 4, 3, 2, 1, 0, 7, 6, 5, 4, 3, 2, 1, 0, -1, -2, 7, 6, 5, 4, 3, 2, -3, -4, -5, -6, 7, 6, -7, -8)
SECOND_ROUTES = ("pz", "zp")
SECOND_ORDER = (0, 1, 0, 1, 0, 1, 1, 0, 0, 1, 0, -1, 1, -2)


def split(value):
    high = value.astype(jnp.bfloat16)
    return high, (value - high.astype(jnp.float32)).astype(jnp.bfloat16)


def split_product(left_high, left_low, right):
    def product(left, right):
        return jnp.dot(left, right, preferred_element_type=jnp.float32)

    high, low = split(right)
    return product(left_low, high) + product(left_high, low) + product(left_high, high)


def plane_sides(chips):
    side = math.isqrt(chips)
    while chips % side:
        side -= 1
    return chips // side, side


class Piece:
    def __init__(self, tiles, order, chips):
        self.used = tiles
        self.tiles = -(-tiles // chips) * chips
        self.order = order
        self.step = 0


def make_plan(basis_columns, block_columns, sizes):
    chips = sizes["plane"] * sizes["z"]
    block = basis_columns // 4
    half = block_columns // 2
    square = block * block // 1024
    corner = half * half // 1024
    diagonal, corner = square - square // 4, corner - corner // 4
    shapes = [2 * diagonal, square, square, square] + [block * half // 1024] * 4
    first = [Piece(tiles, [AXES[letter] for letter in route], chips) for tiles, route in zip(shapes, FIRST_ROUTES)]
    second = [Piece(tiles, [AXES[letter] for letter in route], chips) for tiles, route in zip((corner, half * half // 2048), SECOND_ROUTES)]
    basis_gram, coeffs, gram = first[:4], first[4:], second
    place = dict(copy=0, source=0, held=0, partial=0)
    for group in (basis_gram, coeffs, gram):
        offset = 0
        for piece in group:
            piece.offset = offset
            offset += piece.tiles
            piece.source = place["source"]
            place["source"] += piece.tiles
            piece.stages = []
            size = piece.tiles
            for axis in piece.order:
                count = sizes[axis]
                size //= count
                stage = dict(axis=axis, size=size, held=place["held"], partial=place["partial"])
                stage["scatter"] = place["copy"]
                stage["gather"] = place["copy"] + count - 1
                place["copy"] += 2 * (count - 1)
                place["held"] += (count - 1) * size
                place["partial"] += size
                piece.stages.append(stage)
            piece.partner = place["copy"]
            place["copy"] += 1
    return basis_gram, coeffs, gram, place


def pieces_to_tiles(value):
    rows, cols = value.shape
    return [value[:, i : i + TILE].reshape(rows // 8, 8, TILE) for i in range(0, cols, TILE)]


def orthogonalize_kernel(
    plan,
    sizes,
    weight,
    counts_ref,
    basis_hbm,
    block_hbm,
    residual_hbm,
    gram_ref,
    basis_ref,
    block_ref,
    load_sem,
    store_sem,
    basis_all,
    block_half,
    block_send,
    source,
    held,
    partial,
    basis_gram_tiles,
    coeffs_tiles,
    gram_tiles,
    operator,
    basis_parts,
    correction,
    residual,
    send_sem,
    recv_sem,
    extra_send,
    extra_recv,
):
    basis_gram, coeffs, gram, _ = plan
    slots = basis_ref.shape[0]
    columns = basis_ref.shape[1]
    half = block_ref.shape[1] // 2
    block = columns // 4

    loads = [
        pltpu.make_async_copy(basis_hbm, basis_ref, load_sem.at[0]),
        pltpu.make_async_copy(block_hbm, block_ref, load_sem.at[1]),
    ]
    for copy in loads:
        copy.start()
    row = lax.axis_index("row")
    core = lax.rem(row, 2)
    chip = lax.div(row, 2)
    me = {
        "x": lax.rem(chip, sizes["x"]),
        "y": lax.div(chip, sizes["x"]),
        "z": lax.axis_index("grp"),
        "plane": chip,
        "near": lax.rem(lax.axis_index("grp"), sizes["near"]),
        "far": lax.div(lax.axis_index("grp"), sizes["near"]),
    }
    partner = {"row": row + 1 - 2 * core}

    def peer(axis, k):
        other = lax.rem(me[axis] + k, sizes[axis])
        if axis == "z":
            return {"grp": other}
        if axis == "near":
            return {"grp": me["far"] * sizes["near"] + other}
        if axis == "far":
            return {"grp": other * sizes["near"] + me["near"]}
        if axis == "plane":
            return {"row": other * 2 + core}
        x, y = (other, me["y"]) if axis == "x" else (me["x"], other)
        return {"row": (y * sizes["x"] + x) * 2 + core}

    barrier = pltpu.get_barrier_semaphore()
    pl.semaphore_signal(barrier, inc=1, device_id=partner, device_id_type=MESH)
    for axis in ("plane", "z"):
        for k in range(1, sizes[axis]):
            pl.semaphore_signal(barrier, inc=1, device_id=peer(axis, k), device_id_type=MESH)
    sent = []

    def start(source_ref, target_ref, sends, recvs, device):
        copy = pltpu.make_async_remote_copy(
            src_ref=source_ref,
            dst_ref=target_ref,
            send_sem=sends,
            recv_sem=recvs,
            device_id=device,
            device_id_type=MESH,
        )
        copy.start()
        sent.append(copy)
        return copy

    live = lax.broadcasted_iota(jnp.int32, (slots, 1), 0) < counts_ref[0, 0]
    mine = pl.ds(pl.multiple_of(core * slots, 8), slots)
    near = pl.ds(pl.multiple_of(core * half, TILE), half)
    far = pl.ds(pl.multiple_of((1 - core) * half, TILE), half)
    for copy in loads:
        copy.wait()
    basis_all[mine, :] = jnp.where(live, basis_ref[...], 0.0)
    block_send[...] = jnp.where(live, block_ref[:, far], 0.0)
    block_half[mine, :] = jnp.where(live, block_ref[:, near], 0.0)
    pl.semaphore_wait(barrier, sizes["plane"] + sizes["z"] - 1)
    wide = columns // 2
    shared = []
    for index, side in enumerate((1 - core, core)):
        place = basis_all.at[mine, pl.ds(pl.multiple_of(side * wide, TILE), wide)]
        shared.append(start(place, place, extra_send.at[index], extra_recv.at[index], partner))
    shared.append(start(block_send, block_half.at[mine], extra_send.at[3], extra_recv.at[3], partner))

    def position(piece, depth):
        offset = 0
        for stage in piece.stages[:depth]:
            offset = offset + me[stage["axis"]] * stage["size"]
        return offset

    def scatter(piece, depth):
        stage = piece.stages[depth]
        axis, size = stage["axis"], stage["size"]
        if depth == 0:
            base, ref = piece.source, source
        else:
            base, ref = piece.stages[depth - 1]["partial"], partial
        piece.waiting = []
        for k in range(1, sizes[axis]):
            chunk = lax.rem(me[axis] + k, sizes[axis]) * size
            index = stage["scatter"] + k - 1
            piece.waiting.append(
                start(
                    ref.at[pl.ds(base + chunk, size)],
                    held.at[pl.ds(stage["held"] + (k - 1) * size, size)],
                    send_sem.at[index],
                    recv_sem.at[index],
                    peer(axis, k),
                )
            )

    def reduced(piece, depth):
        stage = piece.stages[depth]
        axis, size = stage["axis"], stage["size"]
        if depth == 0:
            base, ref = piece.source, source
        else:
            base, ref = piece.stages[depth - 1]["partial"], partial
        for copy in piece.waiting:
            copy.wait_recv()
        total = ref[pl.ds(base + me[axis] * size, size)]
        for k in range(sizes[axis] - 1):
            total = total + held[pl.ds(stage["held"] + k * size, size)]
        return total

    def gather(piece, depth):
        stage = piece.stages[depth]
        axis = stage["axis"]
        place = piece.out.at[pl.ds(piece.offset + position(piece, depth + 1), stage["size"])]
        piece.waiting = []
        for k in range(1, sizes[axis]):
            index = stage["gather"] + k - 1
            piece.waiting.append(start(place, place, send_sem.at[index], recv_sem.at[index], peer(axis, k)))

    def stage_source(piece):
        offset = piece.source
        for value in piece.produce():
            source[pl.ds(offset, value.shape[0])] = value
            offset += value.shape[0]
        if piece.used < piece.tiles:
            source[pl.ds(offset, piece.tiles - piece.used)] = jnp.zeros(
                (piece.tiles - piece.used, 8, TILE), jnp.float32
            )

    def advance(piece):
        depth = len(piece.stages)
        step = piece.step
        piece.step += 1
        if step == 0:
            stage_source(piece)
            scatter(piece, 0)
            return
        if step < depth:
            stage = piece.stages[step - 1]
            partial[pl.ds(stage["partial"], stage["size"])] = reduced(piece, step - 1)
            scatter(piece, step)
            return
        if step == depth:
            size = piece.stages[-1]["size"]
            piece.out[pl.ds(piece.offset + position(piece, depth), size)] = reduced(piece, depth - 1)
            gather(piece, depth - 1)
            return
        for copy in piece.waiting:
            copy.wait_recv()
        piece.waiting = []
        if step < 2 * depth:
            gather(piece, 2 * depth - 1 - step)
        elif step == 2 * depth and piece.shared:
            place = piece.out.at[pl.ds(piece.offset, piece.tiles)]
            index = piece.partner
            piece.waiting = [start(place, place, send_sem.at[index], recv_sem.at[index], partner)]

    def run(pieces, order):
        for entry in order:
            if entry < 0:
                pieces[~entry].consume()
            else:
                advance(pieces[entry])

    def lanes(index, width):
        return pl.ds(pl.multiple_of(index * width, TILE), width)

    first, second = 2 * core, 2 * core + 1

    def basis_product(left, right):
        return transposed_product(basis_all[:, lanes(left, block)], basis_all[:, lanes(right, block)]) * weight

    def upper_tiles(value):
        middle = value.shape[0] // 2
        return pieces_to_tiles(value[:middle]) + pieces_to_tiles(value[middle:, middle:])

    def square_at(ref, offset, rows, cols):
        parts = [
            ref[pl.ds(offset + i * (rows // 8), rows // 8)].reshape(rows, TILE) for i in range(cols // TILE)
        ]
        return jnp.concatenate(parts, axis=1)

    def upper_at(ref, offset, size):
        middle = size // 2
        top = square_at(ref, offset, middle, size)
        corner = square_at(ref, offset + middle * size // 1024, middle, middle)
        return top, corner

    square = block * block // 1024

    def put_diagonal(owner, offset, index):
        top, corner = upper_at(basis_gram_tiles.at[owner], offset, block)
        middle = block // 2
        whole = jnp.concatenate([top, jnp.concatenate([top[:, middle:].T, corner], axis=1)], axis=0)
        unit = lax.broadcasted_iota(jnp.int32, whole.shape, 0) == lax.broadcasted_iota(jnp.int32, whole.shape, 1)
        window = slice(index * block, (index + 1) * block)
        operator[0, window, window], operator[1, window, window] = split(jnp.where(unit, 1.0, 0.0) - whole)

    def put_square(owner, offset, left, right):
        whole = -square_at(basis_gram_tiles.at[owner], offset, block, block)
        rows, cols = slice(left * block, (left + 1) * block), slice(right * block, (right + 1) * block)
        operator[0, rows, cols], operator[1, rows, cols] = split(whole)
        operator[0, cols, rows], operator[1, cols, rows] = split(whole.T)

    def consume_diagonals():
        offset = basis_gram[0].offset
        for owner in range(2):
            put_diagonal(owner, offset, 2 * owner)
            put_diagonal(owner, offset + square - square // 4, 2 * owner + 1)

    def consume_square(piece, pairs):
        for owner, (left, right) in enumerate(pairs):
            put_square(owner, piece.offset, left, right)

    def produce_coeffs(index):
        if index == 3:
            basis_parts[0], basis_parts[1] = split(basis_all[...])
        return pieces_to_tiles(
            transposed_product(basis_all[:, index * block : (index + 1) * block], block_half[...]) * weight
        )

    def consume_coeffs(index):
        piece = coeffs[index]
        value = square_at(coeffs_tiles, piece.offset, block, half)
        window = slice(index * block, (index + 1) * block)
        change = split_product(operator[0, :, window], operator[1, :, window], value)
        removed = matrix_product(basis_all[:, window], value)
        if index == 0:
            correction[...] = change
            residual[core] = block_half[...] - removed
        else:
            correction[...] += change
            residual[core] -= removed

    for piece in basis_gram:
        piece.out, piece.shared = basis_gram_tiles.at[core], True
    for piece in coeffs:
        piece.out, piece.shared = coeffs_tiles, False
    for piece in gram:
        piece.out, piece.shared = gram_tiles.at[core], True
    def produce_diagonals():
        shared[0].wait_recv()
        return upper_tiles(basis_product(first, first)) + upper_tiles(basis_product(second, second))

    def produce_beyond():
        shared[1].wait_recv()
        shared[2].wait_recv()
        return pieces_to_tiles(basis_product(second, lax.rem(second + 1, 4)))

    basis_gram[0].produce = produce_diagonals
    basis_gram[1].produce = lambda: pieces_to_tiles(basis_product(first, second))
    basis_gram[2].produce = produce_beyond
    basis_gram[3].produce = lambda: pieces_to_tiles(basis_product(core, core + 2))
    basis_gram[0].consume = consume_diagonals
    basis_gram[1].consume = lambda: consume_square(basis_gram[1], ((0, 1), (2, 3)))
    basis_gram[2].consume = lambda: consume_square(basis_gram[2], ((1, 2), (3, 0)))
    basis_gram[3].consume = lambda: consume_square(basis_gram[3], ((0, 2), (1, 3)))
    for index, piece in enumerate(coeffs):
        piece.produce = functools.partial(produce_coeffs, index)
        piece.consume = functools.partial(consume_coeffs, index)

    run(basis_gram + coeffs, FIRST_ORDER)

    residual[core] -= split_product(basis_parts[0], basis_parts[1], correction[...])
    stores = [
        pltpu.make_async_copy(
            residual.at[owner, mine],
            residual_hbm.at[:, owner * half : (owner + 1) * half],
            store_sem.at[owner],
        )
        for owner in range(2)
    ]
    swap = start(residual.at[core], residual.at[core], extra_send.at[2], extra_recv.at[2], partner)

    gram_ref[...] = jnp.zeros_like(gram_ref)

    def produce_cross():
        swap.wait_recv()
        for copy in stores:
            copy.start()
        left = residual[0, :, lanes(core, half // 2)]
        return pieces_to_tiles(transposed_product(left, residual[1]) * weight)

    def consume_corners():
        for owner in range(2):
            top, corner = upper_at(gram_tiles.at[owner], gram[0].offset, half)
            middle, base = half // 2, owner * half
            gram_ref[base : base + middle, base : base + half] = top
            gram_ref[base + middle : base + half, base + middle : base + half] = corner

    def consume_cross():
        middle = half // 2
        for owner in range(2):
            gram_ref[owner * middle : (owner + 1) * middle, half:] = square_at(
                gram_tiles.at[owner], gram[1].offset, middle, half
            )

    gram[0].produce = lambda: upper_tiles(transposed_product(residual[core], residual[core]) * weight)
    gram[0].consume = consume_corners
    gram[1].produce = produce_cross
    gram[1].consume = consume_cross
    run(gram, SECOND_ORDER)
    for copy in stores:
        copy.wait()
    for copy in sent:
        copy.wait_send()


def orthogonalize(basis, block, counts):
    slots, columns = basis.shape
    width = block.shape[1]
    row_size, grp_size = lax.axis_size("row"), lax.axis_size("grp")
    across, down = plane_sides(row_size // 2)
    near = 2 - grp_size % 2
    sizes = {"x": across, "y": down, "z": grp_size, "plane": across * down, "near": near, "far": grp_size // near}
    plan = make_plan(columns, width, sizes)
    basis_gram, coeffs, gram, place = plan
    weight = 1.0 / (slots * row_size * grp_size)
    half = width // 2
    vmem = pl.BlockSpec(memory_space=pltpu.VMEM)

    def tiles(*shape):
        return pltpu.VMEM(shape + (8, TILE), jnp.float32)

    def total(group):
        return sum(piece.tiles for piece in group)

    return pl.pallas_call(
        functools.partial(orthogonalize_kernel, plan, sizes, weight),
        out_shape=(
            jax.ShapeDtypeStruct((slots, width), jnp.float32),
            jax.ShapeDtypeStruct((width, width), jnp.float32),
        ),
        in_specs=[pl.BlockSpec(memory_space=pltpu.SMEM)] + [pl.BlockSpec(memory_space=pl.ANY)] * 2,
        out_specs=(pl.BlockSpec(memory_space=pl.ANY), vmem),
        scratch_shapes=[
            pltpu.VMEM((slots, columns), jnp.float32),
            pltpu.VMEM((slots, width), jnp.float32),
            pltpu.SemaphoreType.DMA((2,)),
            pltpu.SemaphoreType.DMA((2,)),
            pltpu.VMEM((2 * slots, columns), jnp.float32),
            pltpu.VMEM((2 * slots, half), jnp.float32),
            pltpu.VMEM((slots, half), jnp.float32),
            tiles(place["source"]),
            tiles(place["held"]),
            tiles(place["partial"]),
            tiles(2, total(basis_gram)),
            tiles(total(coeffs)),
            tiles(2, total(gram)),
            pltpu.VMEM((2, columns, columns), jnp.bfloat16),
            pltpu.VMEM((2, 2 * slots, columns), jnp.bfloat16),
            pltpu.VMEM((columns, half), jnp.float32),
            pltpu.VMEM((2, 2 * slots, half), jnp.float32),
            pltpu.SemaphoreType.DMA((place["copy"],)),
            pltpu.SemaphoreType.DMA((place["copy"],)),
            pltpu.SemaphoreType.DMA((4,)),
            pltpu.SemaphoreType.DMA((4,)),
        ],
        compiler_params=pltpu.CompilerParams(collective_id=0, has_side_effects=True),
        name="orthogonalize",
    )(counts, basis, block)


BLOCK = 64
GROUP = 8


def eliminate(square):
    size = square.shape[0]
    count = size // GROUP
    shape = (GROUP, 2 * size)
    sub = lax.broadcasted_iota(jnp.int32, shape, 0)
    lane = lax.broadcasted_iota(jnp.int32, shape, 1)
    wide = [
        jnp.concatenate(
            [
                square[GROUP * b : GROUP * (b + 1)],
                (lane[:, :size] == sub[:, :size] + GROUP * b).astype(jnp.float32),
            ],
            axis=1,
        )
        for b in range(count)
    ]

    def across(value, index):
        return jnp.broadcast_to(value[:, index : index + 1], shape)

    def down(value, index):
        return jnp.broadcast_to(value[index : index + 1], shape)

    roots = []

    def shown(value):
        return jnp.where(lane < 2 * size, value, 0.0)

    home = [shown(across(wide[0], i)) for i in range(GROUP)]
    for g in range(count):
        columns = {b: [across(wide[b], GROUP * g + i) for i in range(GROUP)] for b in range(g + 1, count)}
        columns[g] = home
        if g + 1 < count:
            ahead = {b: [shown(across(wide[b], GROUP * (g + 1) + i)) for i in range(GROUP)] for b in (g, g + 1)}
        pivots = jnp.ones(shape, jnp.float32)
        for i in range(GROUP):
            pivot = down(columns[g][i], i)
            inverse = 1.0 / pivot
            pivots = jnp.where(sub == i, pivot, pivots)
            later = [down(columns[g][j], i) for j in range(i + 1, GROUP)]
            row = down(wide[g], i)
            if g + 1 < count:
                cross = [down(value, i) for value in ahead[g]]
            for b in range(g, count):
                if b == g and i == GROUP - 1:
                    continue
                column = jnp.where(sub > i, columns[b][i], 0.0) if b == g else columns[b][i]
                factor = column * inverse
                for j in range(i + 1, GROUP):
                    columns[b][j] = columns[b][j] - factor * later[j - i - 1]
                wide[b] = wide[b] - factor * row
                if g + 1 < count and b <= g + 1:
                    ahead[b] = [value - factor * over for value, over in zip(ahead[b], cross)]
        if g + 1 < count:
            home = ahead[g + 1]
        roots.append(lax.rsqrt(pivots))
    upper, inverted = [], []
    for b in range(count):
        value = wide[b] * roots[b]
        upper.append(jnp.where((lane >= sub + GROUP * b)[:, :size], value[:, :size], 0.0))
        inverted.append(jnp.where((lane <= sub + GROUP * b)[:, :size], value[:, size:], 0.0))
    return jnp.concatenate(upper, axis=0), jnp.concatenate(inverted, axis=0)


def factor_kernel(gram_hbm, residual_hbm, new_hbm, factor_hbm, work, rest, new_ref, factor_ref, load_sem, store_sem):
    size = gram_hbm.shape[0]
    steps = size // BLOCK
    loads = [
        pltpu.make_async_copy(gram_hbm.at[:BLOCK], work.at[:BLOCK], load_sem.at[0]),
        pltpu.make_async_copy(gram_hbm.at[BLOCK:], work.at[BLOCK:], load_sem.at[1]),
        pltpu.make_async_copy(residual_hbm, rest, load_sem.at[2]),
    ]
    for copy in loads:
        copy.start()
    stores = []

    def store(source, target):
        copy = pltpu.make_async_copy(source, target, store_sem.at[len(stores)])
        copy.start()
        stores.append(copy)

    loads[0].wait()
    square = work[:BLOCK, :BLOCK]
    for step in range(steps):
        here, after, beyond = (BLOCK * (step + i) for i in range(3))
        upper, inverted = eliminate(square)
        if step == 0:
            loads[1].wait()
            loads[2].wait()
        if step:
            factor_ref[here:after, :here] = jnp.zeros((BLOCK, here), jnp.float32)
        factor_ref[here:after, here:after] = upper
        if after < size:
            near = matrix_product(inverted, work[here:after, after:beyond])
            square = work[after:beyond, after:beyond] - transposed_product(near, near)
            factor_ref[here:after, after:beyond] = near
            if beyond < size:
                panel = matrix_product(inverted, work[here:after, beyond:])
                factor_ref[here:after, beyond:] = panel
                work[after:beyond, beyond:] -= transposed_product(near, panel)
                for start in range(beyond, size, 2 * BLOCK):
                    stop = min(start + 2 * BLOCK, size)
                    work[start:stop, start:] -= transposed_product(
                        panel[:, start - beyond : stop - beyond], panel[:, start - beyond :]
                    )
        solved = lax.dot_general(
            rest[:, here:after],
            inverted,
            (((1,), (1,)), ((), ())),
            precision=HIGHEST,
            preferred_element_type=jnp.float32,
        )
        new_ref[:, here:after] = solved
        store(factor_ref.at[here:after], factor_hbm.at[here:after])
        if after % TILE == 0:
            store(new_ref.at[:, after - TILE : after], new_hbm.at[:, after - TILE : after])
        if after < size:
            rest[:, after:] -= matrix_product(solved, factor_ref[here:after, after:])
    for copy in stores:
        copy.wait()


def factor_and_solve(gram, residual):
    hbm = pl.BlockSpec(memory_space=pl.ANY)
    copies = gram.shape[0] // BLOCK + gram.shape[0] // TILE
    return pl.pallas_call(
        factor_kernel,
        out_shape=(
            jax.ShapeDtypeStruct(residual.shape, jnp.float32),
            jax.ShapeDtypeStruct(gram.shape, jnp.float32),
        ),
        in_specs=[hbm, hbm],
        out_specs=(hbm, hbm),
        scratch_shapes=[
            pltpu.VMEM(gram.shape, jnp.float32),
            pltpu.VMEM(residual.shape, jnp.float32),
            pltpu.VMEM(residual.shape, jnp.float32),
            pltpu.VMEM(gram.shape, jnp.float32),
            pltpu.SemaphoreType.DMA((3,)),
            pltpu.SemaphoreType.DMA((copies,)),
        ],
        name="factor_and_solve",
    )(gram, residual)


def body(basis, block, counts):
    residual, gram = orthogonalize(basis, block, counts)
    return factor_and_solve(gram, residual)


def solution(mesh):
    placed = (P(("grp", "row"), None), P(("grp", "row"), None), P("grp", "row"))
    return jax.shard_map(
        body, mesh=mesh, in_specs=placed, out_specs=(P(("grp", "row"), None), P()), check_vma=False
    )
```

```python
import functools
import math

import jax
import jax.numpy as jnp
from jax import lax
from jax.experimental import pallas as pl
from jax.experimental.pallas import tpu as pltpu
from jax.sharding import PartitionSpec as P

HIGHEST = lax.Precision.HIGHEST
MESH = pl.DeviceIdType.MESH
TILE = 128


def transposed_product(left, right):
    return lax.dot_general(
        left,
        right,
        (((0,), (0,)), ((), ())),
        precision=HIGHEST,
        preferred_element_type=jnp.float32,
    )


def matrix_product(left, right):
    return jnp.dot(left, right, precision=HIGHEST, preferred_element_type=jnp.float32)


AXES = {"x": "x", "y": "y", "z": "z", "n": "near", "f": "far", "p": "plane"}
FIRST_ROUTES = ("xyz", "yxz", "zxy", "yxz", "xyz", "yxz", "yxz", "xyz")
FIRST_ORDER = (0, 1, 2, 3, 1, 0, 4, 5, 3, 2, 1, 0, 6, 7, 5, 4, 3, 2, 1, 0, 7, 6, 5, 4, 3, 2, 1, 0, 7, 6, 5, 4, 3, 2, 1, 0, 7, 6, 5, 4, 3, 2, 1, 0, 7, 6, 5, 4, 3, 2, 1, 0, -1, -2, 7, 6, 5, 4, 3, 2, -3, -4, -5, -6, 7, 6, -7, -8)
SECOND_ROUTES = ("pz", "zp")
SECOND_ORDER = (0, 1, 0, 1, 0, 1, 1, 0, 0, 1, 0, -1, 1, -2)


def split(value):
    high = value.astype(jnp.bfloat16)
    return high, (value - high.astype(jnp.float32)).astype(jnp.bfloat16)


def split_product(left_high, left_low, right):
    def product(left, right):
        return jnp.dot(left, right, preferred_element_type=jnp.float32)

    high, low = split(right)
    return product(left_low, high) + product(left_high, low) + product(left_high, high)


def split_fully(value):
    high = value.astype(jnp.bfloat16)
    return (high,) + split(value - high.astype(jnp.float32))


def full_product(left, right, left_axis):
    def product(a, b):
        return lax.dot_general(a, b, (((left_axis,), (0,)), ((), ())), preferred_element_type=jnp.float32)

    small = product(left[1], right[1]) + (product(left[0], right[2]) + product(left[2], right[0]))
    return small + (product(left[0], right[1]) + product(left[1], right[0])) + product(left[0], right[0])


def plane_sides(chips):
    side = math.isqrt(chips)
    while chips % side:
        side -= 1
    return chips // side, side


class Piece:
    def __init__(self, tiles, order, chips):
        self.used = tiles
        self.tiles = -(-tiles // chips) * chips
        self.order = order
        self.step = 0


def make_plan(basis_columns, block_columns, sizes):
    chips = sizes["plane"] * sizes["z"]
    block = basis_columns // 4
    half = block_columns // 2
    square = block * block // 1024
    corner = half * half // 1024
    diagonal, corner = square - square // 4, corner - corner // 4
    shapes = [2 * diagonal, square, square, square] + [block * half // 1024] * 4
    first = [Piece(tiles, [AXES[letter] for letter in route], chips) for tiles, route in zip(shapes, FIRST_ROUTES)]
    second = [Piece(tiles, [AXES[letter] for letter in route], chips) for tiles, route in zip((corner, half * half // 2048), SECOND_ROUTES)]
    basis_gram, coeffs, gram = first[:4], first[4:], second
    place = dict(copy=0, source=0, held=0, partial=0)
    for group in (basis_gram, coeffs, gram):
        offset = 0
        for piece in group:
            piece.offset = offset
            offset += piece.tiles
            piece.source = place["source"]
            place["source"] += piece.tiles
            piece.stages = []
            size = piece.tiles
            for axis in piece.order:
                count = sizes[axis]
                size //= count
                stage = dict(axis=axis, size=size, held=place["held"], partial=place["partial"])
                stage["scatter"] = place["copy"]
                stage["gather"] = place["copy"] + count - 1
                place["copy"] += 2 * (count - 1)
                place["held"] += (count - 1) * size
                place["partial"] += size
                piece.stages.append(stage)
            piece.partner = place["copy"]
            place["copy"] += 1
    return basis_gram, coeffs, gram, place


def pieces_to_tiles(value):
    rows, cols = value.shape
    return [value[:, i : i + TILE].reshape(rows // 8, 8, TILE) for i in range(0, cols, TILE)]


def orthogonalize_kernel(
    plan,
    sizes,
    weight,
    counts_ref,
    basis_hbm,
    block_hbm,
    residual_hbm,
    gram_ref,
    basis_ref,
    block_ref,
    load_sem,
    store_sem,
    basis_all,
    block_half,
    block_send,
    source,
    held,
    partial,
    basis_gram_tiles,
    coeffs_tiles,
    gram_tiles,
    operator,
    basis_parts,
    block_parts,
    correction,
    residual,
    send_sem,
    recv_sem,
    extra_send,
    extra_recv,
):
    basis_gram, coeffs, gram, _ = plan
    slots = basis_ref.shape[0]
    columns = basis_ref.shape[1]
    half = block_ref.shape[1] // 2
    block = columns // 4

    loads = [
        pltpu.make_async_copy(basis_hbm, basis_ref, load_sem.at[0]),
        pltpu.make_async_copy(block_hbm, block_ref, load_sem.at[1]),
    ]
    for copy in loads:
        copy.start()
    row = lax.axis_index("row")
    core = lax.rem(row, 2)
    chip = lax.div(row, 2)
    me = {
        "x": lax.rem(chip, sizes["x"]),
        "y": lax.div(chip, sizes["x"]),
        "z": lax.axis_index("grp"),
        "plane": chip,
        "near": lax.rem(lax.axis_index("grp"), sizes["near"]),
        "far": lax.div(lax.axis_index("grp"), sizes["near"]),
    }
    partner = {"row": row + 1 - 2 * core}

    def peer(axis, k):
        other = lax.rem(me[axis] + k, sizes[axis])
        if axis == "z":
            return {"grp": other}
        if axis == "near":
            return {"grp": me["far"] * sizes["near"] + other}
        if axis == "far":
            return {"grp": other * sizes["near"] + me["near"]}
        if axis == "plane":
            return {"row": other * 2 + core}
        x, y = (other, me["y"]) if axis == "x" else (me["x"], other)
        return {"row": (y * sizes["x"] + x) * 2 + core}

    barrier = pltpu.get_barrier_semaphore()
    pl.semaphore_signal(barrier, inc=1, device_id=partner, device_id_type=MESH)
    for axis in ("plane", "z"):
        for k in range(1, sizes[axis]):
            pl.semaphore_signal(barrier, inc=1, device_id=peer(axis, k), device_id_type=MESH)
    sent = []

    def start(source_ref, target_ref, sends, recvs, device):
        copy = pltpu.make_async_remote_copy(
            src_ref=source_ref,
            dst_ref=target_ref,
            send_sem=sends,
            recv_sem=recvs,
            device_id=device,
            device_id_type=MESH,
        )
        copy.start()
        sent.append(copy)
        return copy

    live = lax.broadcasted_iota(jnp.int32, (slots, 1), 0) < counts_ref[0, 0]
    mine = pl.ds(pl.multiple_of(core * slots, 8), slots)
    near = pl.ds(pl.multiple_of(core * half, TILE), half)
    far = pl.ds(pl.multiple_of((1 - core) * half, TILE), half)
    for copy in loads:
        copy.wait()
    basis_all[mine, :] = jnp.where(live, basis_ref[...], 0.0)
    block_send[...] = jnp.where(live, block_ref[:, far], 0.0)
    block_half[mine, :] = jnp.where(live, block_ref[:, near], 0.0)
    pl.semaphore_wait(barrier, sizes["plane"] + sizes["z"] - 1)
    wide = columns // 2
    shared = []
    for index, side in enumerate((1 - core, core)):
        place = basis_all.at[mine, pl.ds(pl.multiple_of(side * wide, TILE), wide)]
        shared.append(start(place, place, extra_send.at[index], extra_recv.at[index], partner))
    shared.append(start(block_send, block_half.at[mine], extra_send.at[3], extra_recv.at[3], partner))

    def position(piece, depth):
        offset = 0
        for stage in piece.stages[:depth]:
            offset = offset + me[stage["axis"]] * stage["size"]
        return offset

    def scatter(piece, depth):
        stage = piece.stages[depth]
        axis, size = stage["axis"], stage["size"]
        if depth == 0:
            base, ref = piece.source, source
        else:
            base, ref = piece.stages[depth - 1]["partial"], partial
        piece.waiting = []
        for k in range(1, sizes[axis]):
            chunk = lax.rem(me[axis] + k, sizes[axis]) * size
            index = stage["scatter"] + k - 1
            piece.waiting.append(
                start(
                    ref.at[pl.ds(base + chunk, size)],
                    held.at[pl.ds(stage["held"] + (k - 1) * size, size)],
                    send_sem.at[index],
                    recv_sem.at[index],
                    peer(axis, k),
                )
            )

    def reduced(piece, depth):
        stage = piece.stages[depth]
        axis, size = stage["axis"], stage["size"]
        if depth == 0:
            base, ref = piece.source, source
        else:
            base, ref = piece.stages[depth - 1]["partial"], partial
        for copy in piece.waiting:
            copy.wait_recv()
        total = ref[pl.ds(base + me[axis] * size, size)]
        for k in range(sizes[axis] - 1):
            total = total + held[pl.ds(stage["held"] + k * size, size)]
        return total

    def gather(piece, depth):
        stage = piece.stages[depth]
        axis = stage["axis"]
        place = piece.out.at[pl.ds(piece.offset + position(piece, depth + 1), stage["size"])]
        piece.waiting = []
        for k in range(1, sizes[axis]):
            index = stage["gather"] + k - 1
            piece.waiting.append(start(place, place, send_sem.at[index], recv_sem.at[index], peer(axis, k)))

    def stage_source(piece):
        offset = piece.source
        for value in piece.produce():
            source[pl.ds(offset, value.shape[0])] = value
            offset += value.shape[0]
        if piece.used < piece.tiles:
            source[pl.ds(offset, piece.tiles - piece.used)] = jnp.zeros(
                (piece.tiles - piece.used, 8, TILE), jnp.float32
            )

    def advance(piece):
        depth = len(piece.stages)
        step = piece.step
        piece.step += 1
        if step == 0:
            stage_source(piece)
            scatter(piece, 0)
            return
        if step < depth:
            stage = piece.stages[step - 1]
            partial[pl.ds(stage["partial"], stage["size"])] = reduced(piece, step - 1)
            scatter(piece, step)
            return
        if step == depth:
            size = piece.stages[-1]["size"]
            piece.out[pl.ds(piece.offset + position(piece, depth), size)] = reduced(piece, depth - 1)
            gather(piece, depth - 1)
            return
        for copy in piece.waiting:
            copy.wait_recv()
        piece.waiting = []
        if step < 2 * depth:
            gather(piece, 2 * depth - 1 - step)
        elif step == 2 * depth and piece.shared:
            place = piece.out.at[pl.ds(piece.offset, piece.tiles)]
            index = piece.partner
            piece.waiting = [start(place, place, send_sem.at[index], recv_sem.at[index], partner)]

    def run(pieces, order):
        for entry in order:
            if entry < 0:
                pieces[~entry].consume()
            else:
                advance(pieces[entry])

    def lanes(index, width):
        return pl.ds(pl.multiple_of(index * width, TILE), width)

    first, second = 2 * core, 2 * core + 1

    def basis_product(left, right):
        left, right = ([basis_parts[i, :, lanes(side, block)] for i in range(3)] for side in (left, right))
        return full_product(left, right, 0) * weight

    def upper_tiles(value):
        middle = value.shape[0] // 2
        return pieces_to_tiles(value[:middle]) + pieces_to_tiles(value[middle:, middle:])

    def square_at(ref, offset, rows, cols):
        parts = [
            ref[pl.ds(offset + i * (rows // 8), rows // 8)].reshape(rows, TILE) for i in range(cols // TILE)
        ]
        return jnp.concatenate(parts, axis=1)

    def upper_at(ref, offset, size):
        middle = size // 2
        top = square_at(ref, offset, middle, size)
        corner = square_at(ref, offset + middle * size // 1024, middle, middle)
        return top, corner

    square = block * block // 1024

    def put_diagonal(owner, offset, index):
        top, corner = upper_at(basis_gram_tiles.at[owner], offset, block)
        middle = block // 2
        whole = jnp.concatenate([top, jnp.concatenate([top[:, middle:].T, corner], axis=1)], axis=0)
        unit = lax.broadcasted_iota(jnp.int32, whole.shape, 0) == lax.broadcasted_iota(jnp.int32, whole.shape, 1)
        window = slice(index * block, (index + 1) * block)
        operator[0, window, window], operator[1, window, window] = split(jnp.where(unit, 1.0, 0.0) - whole)

    def put_square(owner, offset, left, right):
        whole = -square_at(basis_gram_tiles.at[owner], offset, block, block)
        rows, cols = slice(left * block, (left + 1) * block), slice(right * block, (right + 1) * block)
        operator[0, rows, cols], operator[1, rows, cols] = split(whole)
        operator[0, cols, rows], operator[1, cols, rows] = split(whole.T)

    def consume_diagonals():
        offset = basis_gram[0].offset
        for owner in range(2):
            put_diagonal(owner, offset, 2 * owner)
            put_diagonal(owner, offset + square - square // 4, 2 * owner + 1)

    def consume_square(piece, pairs):
        for owner, (left, right) in enumerate(pairs):
            put_square(owner, piece.offset, left, right)

    def produce_coeffs(index):
        window = slice(index * block, (index + 1) * block)
        return pieces_to_tiles(
            full_product([basis_parts[i, :, window] for i in range(3)], [block_parts[i] for i in range(3)], 0) * weight
        )

    def consume_coeffs(index):
        piece = coeffs[index]
        value = square_at(coeffs_tiles, piece.offset, block, half)
        window = slice(index * block, (index + 1) * block)
        change = split_product(operator[0, :, window], operator[1, :, window], value)
        removed = full_product([basis_parts[i, :, window] for i in range(3)], split_fully(value), 1)
        if index == 0:
            correction[...] = change
            residual[core] = block_half[...] - removed
        else:
            correction[...] += change
            residual[core] -= removed

    for piece in basis_gram:
        piece.out, piece.shared = basis_gram_tiles.at[core], True
    for piece in coeffs:
        piece.out, piece.shared = coeffs_tiles, False
    for piece in gram:
        piece.out, piece.shared = gram_tiles.at[core], True
    def take_basis(side):
        place = pl.ds(pl.multiple_of(side * wide, TILE), wide)
        for i, part in enumerate(split_fully(basis_all[:, place])):
            basis_parts[i, :, place] = part

    def produce_diagonals():
        shared[0].wait_recv()
        take_basis(core)
        return upper_tiles(basis_product(first, first)) + upper_tiles(basis_product(second, second))

    def produce_beyond():
        shared[1].wait_recv()
        shared[2].wait_recv()
        take_basis(1 - core)
        for i, part in enumerate(split_fully(block_half[...])):
            block_parts[i] = part
        return pieces_to_tiles(basis_product(second, lax.rem(second + 1, 4)))

    basis_gram[0].produce = produce_diagonals
    basis_gram[1].produce = lambda: pieces_to_tiles(basis_product(first, second))
    basis_gram[2].produce = produce_beyond
    basis_gram[3].produce = lambda: pieces_to_tiles(basis_product(core, core + 2))
    basis_gram[0].consume = consume_diagonals
    basis_gram[1].consume = lambda: consume_square(basis_gram[1], ((0, 1), (2, 3)))
    basis_gram[2].consume = lambda: consume_square(basis_gram[2], ((1, 2), (3, 0)))
    basis_gram[3].consume = lambda: consume_square(basis_gram[3], ((0, 2), (1, 3)))
    for index, piece in enumerate(coeffs):
        piece.produce = functools.partial(produce_coeffs, index)
        piece.consume = functools.partial(consume_coeffs, index)

    run(basis_gram + coeffs, FIRST_ORDER)

    residual[core] -= split_product(basis_parts[0], basis_parts[1], correction[...])
    stores = [
        pltpu.make_async_copy(
            residual.at[owner, mine],
            residual_hbm.at[:, owner * half : (owner + 1) * half],
            store_sem.at[owner],
        )
        for owner in range(2)
    ]
    swap = start(residual.at[core], residual.at[core], extra_send.at[2], extra_recv.at[2], partner)

    gram_ref[...] = jnp.zeros_like(gram_ref)

    def produce_cross():
        swap.wait_recv()
        for copy in stores:
            copy.start()
        left = residual[0, :, lanes(core, half // 2)]
        return pieces_to_tiles(full_product(split_fully(left), split_fully(residual[1]), 0) * weight)

    def consume_corners():
        for owner in range(2):
            top, corner = upper_at(gram_tiles.at[owner], gram[0].offset, half)
            middle, base = half // 2, owner * half
            gram_ref[base : base + middle, base : base + half] = top
            gram_ref[base + middle : base + half, base + middle : base + half] = corner

    def consume_cross():
        middle = half // 2
        for owner in range(2):
            gram_ref[owner * middle : (owner + 1) * middle, half:] = square_at(
                gram_tiles.at[owner], gram[1].offset, middle, half
            )

    gram[0].produce = lambda: upper_tiles(
        full_product(split_fully(residual[core]), split_fully(residual[core]), 0) * weight
    )
    gram[0].consume = consume_corners
    gram[1].produce = produce_cross
    gram[1].consume = consume_cross
    run(gram, SECOND_ORDER)
    for copy in stores:
        copy.wait()
    for copy in sent:
        copy.wait_send()


def orthogonalize(basis, block, counts):
    slots, columns = basis.shape
    width = block.shape[1]
    row_size, grp_size = lax.axis_size("row"), lax.axis_size("grp")
    across, down = plane_sides(row_size // 2)
    near = 2 - grp_size % 2
    sizes = {"x": across, "y": down, "z": grp_size, "plane": across * down, "near": near, "far": grp_size // near}
    plan = make_plan(columns, width, sizes)
    basis_gram, coeffs, gram, place = plan
    weight = 1.0 / (slots * row_size * grp_size)
    half = width // 2
    vmem = pl.BlockSpec(memory_space=pltpu.VMEM)

    def tiles(*shape):
        return pltpu.VMEM(shape + (8, TILE), jnp.float32)

    def total(group):
        return sum(piece.tiles for piece in group)

    return pl.pallas_call(
        functools.partial(orthogonalize_kernel, plan, sizes, weight),
        out_shape=(
            jax.ShapeDtypeStruct((slots, width), jnp.float32),
            jax.ShapeDtypeStruct((width, width), jnp.float32),
        ),
        in_specs=[pl.BlockSpec(memory_space=pltpu.SMEM)] + [pl.BlockSpec(memory_space=pl.ANY)] * 2,
        out_specs=(pl.BlockSpec(memory_space=pl.ANY), vmem),
        scratch_shapes=[
            pltpu.VMEM((slots, columns), jnp.float32),
            pltpu.VMEM((slots, width), jnp.float32),
            pltpu.SemaphoreType.DMA((2,)),
            pltpu.SemaphoreType.DMA((2,)),
            pltpu.VMEM((2 * slots, columns), jnp.float32),
            pltpu.VMEM((2 * slots, half), jnp.float32),
            pltpu.VMEM((slots, half), jnp.float32),
            tiles(place["source"]),
            tiles(place["held"]),
            tiles(place["partial"]),
            tiles(2, total(basis_gram)),
            tiles(total(coeffs)),
            tiles(2, total(gram)),
            pltpu.VMEM((2, columns, columns), jnp.bfloat16),
            pltpu.VMEM((3, 2 * slots, columns), jnp.bfloat16),
            pltpu.VMEM((3, 2 * slots, half), jnp.bfloat16),
            pltpu.VMEM((columns, half), jnp.float32),
            pltpu.VMEM((2, 2 * slots, half), jnp.float32),
            pltpu.SemaphoreType.DMA((place["copy"],)),
            pltpu.SemaphoreType.DMA((place["copy"],)),
            pltpu.SemaphoreType.DMA((4,)),
            pltpu.SemaphoreType.DMA((4,)),
        ],
        compiler_params=pltpu.CompilerParams(collective_id=0, has_side_effects=True),
        name="orthogonalize",
    )(counts, basis, block)


BLOCK = 64
GROUP = 8


def eliminate(square):
    size = square.shape[0]
    count = size // GROUP
    shape = (GROUP, 2 * size)
    sub = lax.broadcasted_iota(jnp.int32, shape, 0)
    lane = lax.broadcasted_iota(jnp.int32, shape, 1)
    wide = [
        jnp.concatenate(
            [
                square[GROUP * b : GROUP * (b + 1)],
                (lane[:, :size] == sub[:, :size] + GROUP * b).astype(jnp.float32),
            ],
            axis=1,
        )
        for b in range(count)
    ]

    def across(value, index):
        return jnp.broadcast_to(value[:, index : index + 1], shape)

    def down(value, index):
        return jnp.broadcast_to(value[index : index + 1], shape)

    roots = []

    def shown(value):
        return jnp.where(lane < 2 * size, value, 0.0)

    home = [shown(across(wide[0], i)) for i in range(GROUP)]
    for g in range(count):
        columns = {b: [across(wide[b], GROUP * g + i) for i in range(GROUP)] for b in range(g + 1, count)}
        columns[g] = home
        if g + 1 < count:
            ahead = {b: [shown(across(wide[b], GROUP * (g + 1) + i)) for i in range(GROUP)] for b in (g, g + 1)}
        pivots = jnp.ones(shape, jnp.float32)
        for i in range(GROUP):
            pivot = down(columns[g][i], i)
            inverse = 1.0 / pivot
            pivots = jnp.where(sub == i, pivot, pivots)
            later = [down(columns[g][j], i) for j in range(i + 1, GROUP)]
            row = down(wide[g], i)
            if g + 1 < count:
                cross = [down(value, i) for value in ahead[g]]
            for b in range(g, count):
                if b == g and i == GROUP - 1:
                    continue
                column = jnp.where(sub > i, columns[b][i], 0.0) if b == g else columns[b][i]
                factor = column * inverse
                for j in range(i + 1, GROUP):
                    columns[b][j] = columns[b][j] - factor * later[j - i - 1]
                wide[b] = wide[b] - factor * row
                if g + 1 < count and b <= g + 1:
                    ahead[b] = [value - factor * over for value, over in zip(ahead[b], cross)]
        if g + 1 < count:
            home = ahead[g + 1]
        roots.append(lax.rsqrt(pivots))
    upper, inverted = [], []
    for b in range(count):
        value = wide[b] * roots[b]
        upper.append(jnp.where((lane >= sub + GROUP * b)[:, :size], value[:, :size], 0.0))
        inverted.append(jnp.where((lane <= sub + GROUP * b)[:, :size], value[:, size:], 0.0))
    return jnp.concatenate(upper, axis=0), jnp.concatenate(inverted, axis=0)


def factor_kernel(gram_hbm, residual_hbm, new_hbm, factor_hbm, work, rest, new_ref, factor_ref, load_sem, store_sem):
    size = gram_hbm.shape[0]
    steps = size // BLOCK
    loads = [
        pltpu.make_async_copy(gram_hbm.at[:BLOCK], work.at[:BLOCK], load_sem.at[0]),
        pltpu.make_async_copy(gram_hbm.at[BLOCK:], work.at[BLOCK:], load_sem.at[1]),
        pltpu.make_async_copy(residual_hbm, rest, load_sem.at[2]),
    ]
    for copy in loads:
        copy.start()
    stores = []

    def store(source, target):
        copy = pltpu.make_async_copy(source, target, store_sem.at[len(stores)])
        copy.start()
        stores.append(copy)

    loads[0].wait()
    square = work[:BLOCK, :BLOCK]
    for step in range(steps):
        here, after, beyond = (BLOCK * (step + i) for i in range(3))
        upper, inverted = eliminate(square)
        if step == 0:
            loads[1].wait()
            loads[2].wait()
        if step:
            factor_ref[here:after, :here] = jnp.zeros((BLOCK, here), jnp.float32)
        factor_ref[here:after, here:after] = upper
        if after < size:
            near = matrix_product(inverted, work[here:after, after:beyond])
            square = work[after:beyond, after:beyond] - transposed_product(near, near)
            factor_ref[here:after, after:beyond] = near
            if beyond < size:
                panel = matrix_product(inverted, work[here:after, beyond:])
                factor_ref[here:after, beyond:] = panel
                work[after:beyond, beyond:] -= transposed_product(near, panel)
                for start in range(beyond, size, 2 * BLOCK):
                    stop = min(start + 2 * BLOCK, size)
                    work[start:stop, start:] -= transposed_product(
                        panel[:, start - beyond : stop - beyond], panel[:, start - beyond :]
                    )
        solved = lax.dot_general(
            rest[:, here:after],
            inverted,
            (((1,), (1,)), ((), ())),
            precision=HIGHEST,
            preferred_element_type=jnp.float32,
        )
        new_ref[:, here:after] = solved
        store(factor_ref.at[here:after], factor_hbm.at[here:after])
        if after % TILE == 0:
            store(new_ref.at[:, after - TILE : after], new_hbm.at[:, after - TILE : after])
        if after < size:
            rest[:, after:] -= matrix_product(solved, factor_ref[here:after, after:])
    for copy in stores:
        copy.wait()


def factor_and_solve(gram, residual):
    hbm = pl.BlockSpec(memory_space=pl.ANY)
    copies = gram.shape[0] // BLOCK + gram.shape[0] // TILE
    return pl.pallas_call(
        factor_kernel,
        out_shape=(
            jax.ShapeDtypeStruct(residual.shape, jnp.float32),
            jax.ShapeDtypeStruct(gram.shape, jnp.float32),
        ),
        in_specs=[hbm, hbm],
        out_specs=(hbm, hbm),
        scratch_shapes=[
            pltpu.VMEM(gram.shape, jnp.float32),
            pltpu.VMEM(residual.shape, jnp.float32),
            pltpu.VMEM(residual.shape, jnp.float32),
            pltpu.VMEM(gram.shape, jnp.float32),
            pltpu.SemaphoreType.DMA((3,)),
            pltpu.SemaphoreType.DMA((copies,)),
        ],
        name="factor_and_solve",
    )(gram, residual)


def body(basis, block, counts):
    residual, gram = orthogonalize(basis, block, counts)
    return factor_and_solve(gram, residual)


def solution(mesh):
    placed = (P(("grp", "row"), None), P(("grp", "row"), None), P("grp", "row"))
    return jax.shard_map(
        body, mesh=mesh, in_specs=placed, out_specs=(P(("grp", "row"), None), P()), check_vma=False
    )
```
